32 devices in a mesh: groups: 2 (over y), ctx: 4 (over z), head: 4 (over x, core).
Axes of the slice: x: 2, y: 2, z: 4, core: 2. Of those that a mesh axis runs over, the one named last changes fastest.
Arguments:
- queries: bfloat16 [32768, 2048], P(('groups', 'ctx'), 'head'), parts along dimension 0, may hold values from -6 to 6
- key_vectors: bfloat16 [32768, 2048], P(('groups', 'ctx'), 'head'), parts along dimension 0, may hold values from -0.52734375 to 0.52734375
- value_vectors: bfloat16 [32768, 2048], P(('groups', 'ctx'), 'head'), parts along dimension 0, may hold values from -6 to 6
- token_rows: int32 [32768], P(('groups', 'ctx')), parts along dimension 0, may hold values from 0 to 63
- weight_table: float32 [64, 16, 21], P(None, 'head'), may hold values from 0.1 to 1
Outputs:
- attended: bfloat16 [32768, 2048], P(('groups', 'ctx'), 'head'), parts along dimension 0
The draws below stay inside these ranges and needn't reach their ends.
There are 2 independent parts, one for each index of `groups`. The reference program is written for one: setup_inputs(seed, part) draws one part's arguments, and reference() takes and returns one part's arrays. A program takes and returns all parts, laid end to end along the dimension named above; an argument that names none is the same for every part. Nothing has to cross between parts.
All inputs are finite; a program needn't handle non-finite values.
Results may differ from the reference program's by a relative error of at most 0.004.
Values sent between devices are 32-bit elements; how exact they have to be, the bound alone decides.
No kernel may reach another device: no remote copies, remote signals or barrier semaphores. Data moves between devices by JAX's collectives and lax.ppermute only.
A program may use at most 128 MiB of HBM per device.

```python
import math
import jax
import jax.numpy as jnp
from jax import lax

HEADS = 16
HEAD_DIM = 128
BLOCK = 256
LEVELS = 21
TABLE_ROWS = 64
TOKENS = 16384


def plant(result, stream_key, smallest, high):
    dims = result.shape
    index_at = [jax.random.randint(jax.random.fold_in(stream_key, axis), (), 0, dims[axis]) for axis in range(len(dims))]
    result = result.at[tuple(index_at)].set(smallest)
    longest = dims.index(max(dims))
    index_at[longest] = (index_at[longest] + 1) % dims[longest]
    return result.at[tuple(index_at)].set(high)


def steps_of(own_key, dims, pieces, low, high):
    level, own = 1.0, jax.random.fold_in(own_key, 6)
    for dim, shards_of in pieces:
        heights = jnp.exp(jax.random.uniform(jax.random.fold_in(own, dim), (shards_of,), jnp.float32, low / len(pieces), high / len(pieces)))
        level = level * jnp.repeat(heights, dims[dim] // shards_of).reshape([-1 if axis == dim else 1 for axis in range(len(dims))])
    return level


def scatter_about(stream_key, dims, scale, limit, split=(), kind=jnp.bfloat16):
    level = steps_of(stream_key, dims, split, -0.22, 0.18) if split else 1.0
    values = jax.random.normal(stream_key, dims, jnp.float32) * scale * level
    return jnp.minimum(jnp.maximum(values, -limit), limit).astype(kind)


def setup_inputs(seed: int = 0, part: int = 0) -> dict:
    streams_of = jax.random.split(jax.random.key(seed), 6)
    part_keys = jax.random.split(jax.random.fold_in(streams_of[5], part), 6)
    return {
        "queries": scatter_about(part_keys[0], (TOKENS, HEADS * HEAD_DIM), 1.0, 6.0, ((0, 4), (1, 4))),
        "key_vectors": scatter_about(part_keys[1], (TOKENS, HEADS * HEAD_DIM), (HEAD_DIM ** -0.5), 0.52734375, ((0, 4), (1, 4))),
        "value_vectors": scatter_about(part_keys[2], (TOKENS, HEADS * HEAD_DIM), 1.0, 6.0, ((0, 4), (1, 4))),
        "token_rows": plant(jax.random.randint(part_keys[3], (TOKENS,), 0, TABLE_ROWS), jax.random.fold_in(part_keys[3], 1), 0, TABLE_ROWS - 1).astype(jnp.int32),
        "weight_table": jnp.clip(jnp.exp(math.log(1.0) - 2.3025851 * jax.random.uniform(streams_of[4], (TABLE_ROWS, HEADS, LEVELS), jnp.float32) ** steps_of(streams_of[4], (TABLE_ROWS, HEADS, LEVELS), ((1, 4),), -0.2, 0.2)), 0.1, 1.0),
    }


def level_scale(level_count):
    level_ids = jnp.arange(level_count).astype(jnp.float32)
    return jnp.where(level_ids < 0.5, 1.0, 2.0 ** (-(level_ids - 1.0) / 2.0)).astype(jnp.float32)


def pair_levels(block_rows, block_bits):
    positions = jnp.arange(block_rows, dtype=jnp.int32)
    differing = jnp.bitwise_xor(positions[:, None], positions[None, :])
    pair_level = jnp.zeros((block_rows, block_rows), jnp.int32)
    for level_bit in range(block_bits):
        pair_level = pair_level + (differing >= 2 ** level_bit).astype(jnp.int32)
    pair_level = jnp.where(positions[None, :] <= positions[:, None], pair_level, -1)
    level_ids = jnp.arange(block_bits + 1, dtype=jnp.int32)
    return (pair_level[:, :, None] == level_ids[None, None, :]).astype(jnp.float32)


def reference(queries, key_vectors, value_vectors, token_rows, weight_table):
    token_count = queries.shape[0]
    block_rows = BLOCK
    block_count = token_count // block_rows
    block_bits = block_rows.bit_length() - 1
    all_bits = token_count.bit_length() - 1
    level_weight = weight_table[token_rows] * level_scale(LEVELS)[None, None, :]
    query_blocks = queries.astype(jnp.float32).reshape(block_count, block_rows, HEADS, HEAD_DIM)
    key_blocks = key_vectors.astype(jnp.float32).reshape(block_count, block_rows, HEADS, HEAD_DIM)
    value_blocks = value_vectors.astype(jnp.float32).reshape(block_count, block_rows, HEADS, HEAD_DIM)
    weight_blocks = level_weight.reshape(block_count, block_rows, HEADS, LEVELS)
    level_pick = pair_levels(block_rows, block_bits)

    def inside(block_index):
        query_one = query_blocks[block_index]
        key_one = key_blocks[block_index]
        value_one = value_blocks[block_index]
        weights_one = weight_blocks[block_index]
        pair_weight = jnp.einsum("thl,tsl->hts", weights_one[:, :, :block_bits + 1], level_pick,
                                 precision=lax.Precision.HIGHEST)
        scores = jnp.einsum("thd,shd->hts", query_one, key_one, precision=lax.Precision.HIGHEST)
        weighted = (scores * pair_weight).astype(jnp.bfloat16)
        weighted = lax.optimization_barrier(weighted).astype(jnp.float32)
        return jnp.einsum("hts,shd->thd", weighted, value_one, precision=lax.Precision.HIGHEST)

    result_sum = lax.map(inside, jnp.arange(block_count))
    block_states = jnp.einsum("bshd,bshe->bhde", key_blocks, value_blocks, precision=lax.Precision.HIGHEST)
    for level_bit in range(all_bits - block_bits):
        level_id = block_bits + 1 + level_bit
        span_blocks = 2 ** level_bit
        group_count = block_count // (2 * span_blocks)
        left_sum = block_states.reshape(group_count, 2, span_blocks, HEADS, HEAD_DIM, HEAD_DIM)[:, 0].sum(axis=1)
        right_query = query_blocks.reshape(group_count, 2, span_blocks * block_rows, HEADS, HEAD_DIM)[:, 1]
        product = jnp.einsum("gthd,ghde->gthe", right_query, left_sum, precision=lax.Precision.HIGHEST)
        right_weight = weight_blocks.reshape(group_count, 2, span_blocks * block_rows, HEADS, LEVELS)[:, 1, :, :, level_id]
        result_sum = result_sum.reshape(group_count, 2, span_blocks * block_rows, HEADS, HEAD_DIM)
        result_sum = result_sum.at[:, 1].add(right_weight[..., None] * product)
    return result_sum.reshape(token_count, HEADS * HEAD_DIM).astype(jnp.bfloat16)
```

```python
import jax
import jax.numpy as jnp
from jax import lax
from jax.experimental import pallas as pl
from jax.experimental.pallas import tpu as pltpu
from jax.sharding import PartitionSpec as P

BLOCK = 256
HALF = BLOCK // 2
LANES = 128
SLOT = 32
MIB = 1 << 20


def level_scale(level_count):
    level_ids = jnp.arange(level_count).astype(jnp.float32)
    return jnp.where(level_ids < 0.5, 1.0, 2.0 ** (-(level_ids - 1.0) / 2.0)).astype(jnp.float32)


def pick_table(weight_table):
    rows, heads, levels = weight_table.shape
    scaled = weight_table * level_scale(levels)[None, None, :]
    scaled = jnp.pad(scaled, ((0, 0), (0, 0), (0, SLOT - levels))).reshape(rows, heads * SLOT)
    scaled = jnp.pad(scaled, ((0, 0), (0, LANES - heads * SLOT)))
    high = scaled.astype(jnp.bfloat16)
    low = (scaled - high.astype(jnp.float32)).astype(jnp.bfloat16)
    return jnp.concatenate([high, low], axis=0)


def totals_kernel(key_ref, value_ref, left_ref, total_ref):
    block_count = key_ref.shape[0] // BLOCK
    held = {}
    for block in range(block_count):
        rows = slice(block * BLOCK, (block + 1) * BLOCK)
        carry = lax.dot_general(
            key_ref[rows, :], value_ref[rows, :], (((0,), (0,)), ((), ())),
            preferred_element_type=jnp.float32,
        )
        bit = 0
        while block >> bit & 1:
            carry = carry + held.pop(bit)
            bit += 1
        held[bit] = carry
        if block + 1 < block_count:
            left_ref[0, block] = carry.astype(jnp.bfloat16)
        else:
            total_ref[0] = carry


def local_kernel(rows_ref, table_ref, query_ref, key_ref, value_ref, left_ref, part_ref, weight_ref):
    token_count = query_ref.shape[0]
    block_count = token_count // BLOCK
    block_bits = BLOCK.bit_length() - 1
    head = pl.program_id(0)
    base = head * SLOT

    @pl.when(head == 0)
    def _():
        pair_rows = table_ref.shape[0]
        ids = lax.broadcasted_iota(jnp.int32, (pair_rows, BLOCK), 0) & (pair_rows // 2 - 1)
        for block in range(block_count):
            rows = rows_ref[:, block * BLOCK : (block + 1) * BLOCK]
            pick = (ids == rows).astype(jnp.float32).astype(jnp.bfloat16)
            weight_ref[block * BLOCK : (block + 1) * BLOCK, :] = lax.dot_general(
                pick, table_ref[...], (((0,), (0,)), ((), ())), preferred_element_type=jnp.float32
            )

    target = lax.broadcasted_iota(jnp.int32, (HALF, HALF), 0)
    source = lax.broadcasted_iota(jnp.int32, (HALF, HALF), 1)
    differing = target ^ source
    level = jnp.zeros((HALF, HALF), jnp.int32)
    for bit in range(block_bits - 1):
        level = level + (differing >= 2**bit).astype(jnp.int32)
    level = jnp.where(source <= target, level, SLOT - 1) + base

    def lane(weights, level_id):
        index = jnp.full(weights.shape, level_id, jnp.int32) + base
        return jnp.take_along_axis(weights, index, axis=1, mode="promise_in_bounds")

    for block in range(block_count):
        start = block * BLOCK
        low = slice(start, start + HALF)
        high = slice(start + HALF, start + BLOCK)
        key_all = key_ref[start : start + BLOCK, :]
        value_all = value_ref[start : start + BLOCK, :]
        bits = [bit for bit in range(block_count.bit_length() - 1) if block >> bit & 1]
        lefts = [left_ref[0, (block >> bit << bit) - 1] for bit in bits]

        def finish(rows, weighted, values):
            weights = weight_ref[rows, :]
            query = query_ref[rows, :].astype(jnp.float32)
            parts = [weighted]
            for bit in bits:
                parts.append((query * lane(weights, block_bits + 1 + bit)).astype(jnp.bfloat16))
            left = jnp.concatenate(parts, axis=1) if bits else weighted
            right = jnp.concatenate([values] + lefts, axis=0) if bits else values
            part_ref[rows, :] = jnp.dot(left, right, preferred_element_type=jnp.float32).astype(part_ref.dtype)

        contract = (((1,), (1,)), ((), ()))
        weights = weight_ref[low, :]
        scores = lax.dot_general(
            query_ref[low, :], key_all[:HALF], contract, preferred_element_type=jnp.float32
        )
        own = jnp.take_along_axis(weights, level, axis=1, mode="promise_in_bounds")
        finish(low, (scores * own).astype(jnp.bfloat16), value_all[:HALF])

        weights = weight_ref[high, :]
        scores = lax.dot_general(
            query_ref[high, :], key_all, contract, preferred_element_type=jnp.float32
        )
        own = jnp.take_along_axis(weights, level, axis=1, mode="promise_in_bounds")
        across = lane(weights, block_bits)
        weighted = jnp.concatenate(
            [
                (scores[:, :HALF] * across).astype(jnp.bfloat16),
                (scores[:, HALF:] * own).astype(jnp.bfloat16),
            ],
            axis=1,
        )
        finish(high, weighted, value_all)


def remote_kernel(counts, local_bits, *refs):
    query_ref, weight_ref, part_ref = refs[:3]
    state_refs = refs[3:-1]
    out_ref = refs[-1]
    head = pl.program_id(0)
    base = head * SLOT
    states = []
    place = 0
    for count in counts:
        total = state_refs[place][0]
        for extra in range(1, count):
            total = total + state_refs[place + extra][0]
        states.append(total.astype(jnp.bfloat16))
        place += count
    for start in range(0, query_ref.shape[0], BLOCK):
        rows = slice(start, start + BLOCK)
        weights = weight_ref[rows, :]
        result = part_ref[rows, :].astype(jnp.float32)
        for first in range(0, len(states), 2):
            pair = states[first : first + 2]
            product = jnp.dot(
                query_ref[rows, :], jnp.concatenate(pair, axis=1), preferred_element_type=jnp.float32
            )
            for offset in range(len(pair)):
                index = jnp.full(weights.shape, local_bits + 1 + first + offset, jnp.int32) + base
                scale = jnp.take_along_axis(weights, index, axis=1, mode="promise_in_bounds")
                result = result + scale * product[:, offset * LANES : (offset + 1) * LANES]
        out_ref[rows, :] = result.astype(out_ref.dtype)


def remote_states(total, device_count):
    levels = []
    carry = total
    for bit in range(device_count.bit_length() - 1):
        half = 2**bit
        bases = range(0, device_count, 2 * half)
        arrived = [lax.ppermute(carry, "ctx", [(base + half - 1, base + half) for base in bases])]
        for lower in reversed(range(bit)):
            step = 2**lower
            held = arrived[0]
            for more in arrived[1:]:
                held = held + more
            pairs = [
                (base + half + place, base + half + place + step)
                for base in bases
                for place in range(0, half, 2 * step)
            ]
            arrived.append(lax.ppermute(held, "ctx", pairs))
        levels.append(arrived)
        if 2 * half < device_count:
            for more in arrived[: 1 if bit == 0 else None]:
                carry = carry + more
    return levels


def body(queries, key_vectors, value_vectors, token_rows, weight_table):
    head_count = weight_table.shape[1]
    token_count = queries.shape[0]
    width = queries.shape[1] // head_count
    block_count = token_count // BLOCK
    local_bits = token_count.bit_length() - 1
    column = pl.BlockSpec((token_count, width), lambda head: (0, head))
    state = pl.BlockSpec((1, width, width), lambda head: (head, 0, 0))
    left = pl.BlockSpec((1, block_count, width, width), lambda head: (head, 0, 0, 0))
    params = pltpu.CompilerParams(vmem_limit_bytes=24 * MIB)

    lefts, total = pl.pallas_call(
        totals_kernel,
        grid=(head_count,),
        in_specs=[column, column],
        out_specs=[left, state],
        out_shape=[
            jax.ShapeDtypeStruct((head_count, block_count, width, width), jnp.bfloat16),
            jax.ShapeDtypeStruct((head_count, width, width), jnp.float32),
        ],
        compiler_params=params,
        name="totals",
    )(key_vectors, value_vectors)
    levels = remote_states(total, lax.axis_size("ctx"))

    table = pick_table(weight_table)
    fixed = pl.BlockSpec((token_count, LANES), lambda head: (0, 0))
    partial, weights = pl.pallas_call(
        local_kernel,
        grid=(head_count,),
        in_specs=[
            pl.BlockSpec((1, token_count), lambda head: (0, 0)),
            pl.BlockSpec(table.shape, lambda head: (0, 0)),
            column,
            column,
            column,
            left,
        ],
        out_specs=[column, fixed],
        out_shape=[
            jax.ShapeDtypeStruct(queries.shape, jnp.float32),
            jax.ShapeDtypeStruct((token_count, LANES), jnp.float32),
        ],
        compiler_params=params,
        name="local",
    )(token_rows[None, :], table, queries, key_vectors, value_vectors, lefts)

    counts = tuple(len(arrived) for arrived in levels)
    arrays = [array for arrived in levels for array in arrived]
    return pl.pallas_call(
        lambda *refs: remote_kernel(counts, local_bits, *refs),
        grid=(head_count,),
        in_specs=[column, fixed, column] + [state] * len(arrays),
        out_specs=column,
        out_shape=jax.ShapeDtypeStruct(queries.shape, queries.dtype),
        compiler_params=params,
        name="remote",
    )(queries, weights, partial, *arrays)


def solution(mesh):
    placed = (
        P(("groups", "ctx"), "head"),
        P(("groups", "ctx"), "head"),
        P(("groups", "ctx"), "head"),
        P(("groups", "ctx")),
        P(None, "head", None),
    )
    return jax.shard_map(
        body, mesh=mesh, in_specs=placed, out_specs=P(("groups", "ctx"), "head"), check_vma=False
    )
```

```python
import jax
import jax.numpy as jnp
from jax import lax
from jax.experimental import pallas as pl
from jax.experimental.pallas import tpu as pltpu
from jax.sharding import PartitionSpec as P

BLOCK = 256
HALF = BLOCK // 2
BLOCK_BITS = BLOCK.bit_length() - 1
ROWS = 8
LANES = 128
SLOT = 32
PIECES = 4
MIB = 1 << 20
VMEM = pl.BlockSpec(memory_space=pltpu.VMEM)
HBM = pl.BlockSpec(memory_space=pltpu.HBM)
ANY = pl.BlockSpec(memory_space=pl.ANY)


def columns(head):
    return pl.ds(head * LANES, LANES)


def totals_kernel(heads, extra, *refs):
    key_hbm, value_hbm = refs[:2]
    refs = refs[2:]
    if extra is not None:
        query_hbm = refs[0]
        refs = refs[1:]
    key_ref, value_ref, left_ref, total_ref = refs[:4]
    sems = refs[-1]
    count = len(heads)
    token_count = key_ref.shape[1]
    block_count = token_count // BLOCK
    size = token_count // PIECES
    copies = {}
    for place, head in enumerate(heads):
        for piece in range(PIECES):
            rows = pl.ds(piece * size, size)
            for which, (source, target) in enumerate(((key_hbm, key_ref), (value_hbm, value_ref))):
                copies[place, piece, which] = pltpu.make_async_copy(
                    source.at[rows, columns(head)],
                    target.at[place, rows, :],
                    sems.at[(place * PIECES + piece) * 2 + which],
                )
                copies[place, piece, which].start()
    if extra is not None:
        ahead = pltpu.make_async_copy(
            query_hbm.at[:, columns(extra)], refs[4], sems.at[count * PIECES * 2]
        )
        ahead.start()
    for place in range(count):
        held = {}
        for block in range(block_count):
            if block % (block_count // PIECES) == 0:
                for which in range(2):
                    copies[place, block // (block_count // PIECES), which].wait()
            rows = slice(block * BLOCK, (block + 1) * BLOCK)
            carry = lax.dot_general(
                key_ref[place, rows, :], value_ref[place, rows, :], (((0,), (0,)), ((), ())),
                preferred_element_type=jnp.float32,
            )
            bit = 0
            while block >> bit & 1:
                carry = carry + held.pop(bit)
                bit += 1
            held[bit] = carry
            if block + 1 < block_count:
                left_ref[place, block] = carry.astype(jnp.bfloat16)
            else:
                total_ref[place] = carry
    if extra is not None:
        ahead.wait()


def weights_kernel(rows_ref, table_ref, after_ref, weight_ref, short_ref):
    token_count = weight_ref.shape[0]
    levels, heads, table_rows = table_ref.shape
    level = lax.broadcasted_iota(jnp.int32, (levels, table_rows), 0)
    scale = jnp.ones((levels, table_rows), jnp.float32)
    for level_id in range(2, levels):
        scale = jnp.where(level == level_id, 2.0 ** (-(level_id - 1) / 2), scale)
    slots = []
    for head in range(heads):
        slots.append(table_ref[:, head, :] * scale)
        slots.append(jnp.zeros((SLOT - levels, table_rows), jnp.float32))
    if heads * SLOT < LANES:
        slots.append(jnp.zeros((LANES - heads * SLOT, table_rows), jnp.float32))
    table = jnp.concatenate(slots, axis=0)
    high = table.astype(jnp.bfloat16)
    low = (table - high.astype(jnp.float32)).astype(jnp.bfloat16)
    ids = lax.broadcasted_iota(jnp.int32, (table_rows, BLOCK), 0)
    contract = (((0,), (1,)), ((), ()))
    for start in range(0, token_count, BLOCK):
        pick = (ids == rows_ref[:, start : start + BLOCK]).astype(jnp.float32).astype(jnp.bfloat16)
        weights = lax.dot_general(
            pick, high, contract, preferred_element_type=jnp.float32
        ) + lax.dot_general(pick, low, contract, preferred_element_type=jnp.float32)
        weight_ref[start : start + BLOCK, :] = weights
        short_ref[start : start + BLOCK, :] = weights.astype(jnp.bfloat16)


def join_kernel(*refs):
    total = refs[0][...]
    for ref in refs[1:-1]:
        total = total + ref[...]
    refs[-1][...] = total


def join(arrays):
    if len(arrays) == 1:
        return arrays[0]
    return pl.pallas_call(
        join_kernel,
        in_specs=[VMEM] * len(arrays),
        out_specs=VMEM,
        out_shape=jax.ShapeDtypeStruct(arrays[0].shape, arrays[0].dtype),
        compiler_params=pltpu.CompilerParams(vmem_limit_bytes=2 * MIB),
        name="join",
    )(*arrays)


def gather(weights, index):
    return jnp.take_along_axis(weights, index, axis=1, mode="promise_in_bounds")


def spread(weights, lane):
    return jnp.broadcast_to(weights[:, lane : lane + 1], (weights.shape[0], LANES))


def local_kernel(head, place, follow, *refs):
    query_ref, key_ref, value_ref, left_ref, weight_ref, short_ref = refs[:6]
    refs = refs[6:]
    if follow is not None:
        ahead = pltpu.make_async_copy(refs[0].at[:, columns(follow)], refs[2], refs[3])
        ahead.start()
        part_ref = refs[1]
    else:
        part_ref = refs[0]
    token_count = query_ref.shape[0]
    block_count = token_count // BLOCK
    base = head * SLOT

    target = lax.broadcasted_iota(jnp.int32, (HALF, HALF), 0)
    source = lax.broadcasted_iota(jnp.int32, (HALF, HALF), 1)
    differing = target ^ source
    level = jnp.zeros((HALF, HALF), jnp.int32)
    for bit in range(BLOCK_BITS - 1):
        level = level + (differing >= 2**bit).astype(jnp.int32)
    level = jnp.where(source <= target, level, SLOT - 1) + base

    for block in range(block_count):
        start = block * BLOCK
        rows = slice(start, start + BLOCK)
        query = query_ref[rows, :]
        value = value_ref[place, rows, :]
        scores = lax.dot_general(
            query, key_ref[place, rows, :], (((1,), (1,)), ((), ())),
            preferred_element_type=jnp.float32,
        )
        low, high, across = [], [], []
        for first in range(0, HALF, ROWS):
            index = level[first : first + ROWS]
            below = start + first
            above = below + HALF
            low.append(gather(weight_ref[below : below + ROWS, :], index))
            high.append(gather(weight_ref[above : above + ROWS, :], index))
        across = spread(weight_ref[start + HALF : start + BLOCK, :], base + BLOCK_BITS)
        low = (scores[:HALF, :HALF] * jnp.concatenate(low, axis=0)).astype(jnp.bfloat16)
        high = (scores[HALF:, HALF:] * jnp.concatenate(high, axis=0)).astype(jnp.bfloat16)
        across = (scores[HALF:, :HALF] * across).astype(jnp.bfloat16)
        left = [
            jnp.concatenate([low, across], axis=0),
            jnp.concatenate([jnp.zeros_like(low), high], axis=0),
        ]
        right = [value]
        short = short_ref[rows, :]
        for bit in range(block_count.bit_length() - 1):
            if block >> bit & 1:
                left.append(query * spread(short, base + BLOCK_BITS + 1 + bit))
                right.append(left_ref[place, (block >> bit << bit) - 1])
        part_ref[rows, :] = jnp.dot(
            jnp.concatenate(left, axis=1), jnp.concatenate(right, axis=0),
            preferred_element_type=jnp.float32,
        )
    if follow is not None:
        ahead.wait()


def remote_kernel(heads, counts, local_bits, chained, *refs):
    short_ref = refs[0]
    query_refs = refs[1 : 1 + len(heads)]
    part_refs = refs[1 + len(heads) : 1 + 2 * len(heads)]
    state_refs = refs[1 + 2 * len(heads) : 1 + 2 * len(heads) + sum(counts)]
    out_hbm, buffer, sems = refs[-3:]
    token_count = short_ref.shape[0]
    size = token_count // PIECES
    copies = []
    for place, head in enumerate(heads):
        states = []
        spot = 0
        for count in counts:
            total = state_refs[spot][place]
            for more in range(1, count):
                total = total + state_refs[spot + more][place]
            states.append(total.astype(jnp.bfloat16))
            spot += count
        states = jnp.concatenate(states, axis=0)
        for start in range(0, token_count, BLOCK):
            rows = slice(start, start + BLOCK)
            query = query_refs[place][rows, :]
            short = short_ref[rows, :]
            left = [
                query * spread(short, head * SLOT + local_bits + 1 + bit)
                for bit in range(len(counts))
            ]
            result = part_refs[place][rows, :] + jnp.dot(
                jnp.concatenate(left, axis=1), states, preferred_element_type=jnp.float32
            )
            buffer[place, rows, :] = result.astype(buffer.dtype)
            if (start + BLOCK) % size == 0:
                piece = pl.ds(start + BLOCK - size, size)
                copies.append(
                    pltpu.make_async_copy(
                        buffer.at[place, piece, :], out_hbm.at[piece, columns(head)], sems.at[len(copies)]
                    )
                )
                copies[-1].start()
    for copy in copies:
        copy.wait()


def remote_states(total, device_count):
    levels = []
    carry = total
    for bit in range(device_count.bit_length() - 1):
        half = 2**bit
        bases = range(0, device_count, 2 * half)
        arrived = [lax.ppermute(carry, "ctx", [(base + half - 1, base + half) for base in bases])]
        for lower in reversed(range(bit)):
            step = 2**lower
            held = join(arrived)
            pairs = [
                (base + half + place, base + half + place + step)
                for base in bases
                for place in range(0, half, 2 * step)
            ]
            arrived.append(lax.ppermute(held, "ctx", pairs))
        levels.append(arrived)
        if 2 * half < device_count:
            carry = join([carry] + arrived)
    return levels


def body(queries, key_vectors, value_vectors, token_rows, weight_table):
    head_count = weight_table.shape[1]
    token_count = queries.shape[0]
    width = queries.shape[1] // head_count
    block_count = token_count // BLOCK
    local_bits = token_count.bit_length() - 1
    group = head_count // 2
    shape = jax.ShapeDtypeStruct
    whole = shape((token_count, width), jnp.bfloat16)
    params = pltpu.CompilerParams(vmem_limit_bytes=8 * MIB)

    queries, key_vectors, value_vectors = (
        pltpu.with_memory_space_constraint(array, pltpu.HBM) for array in (queries, key_vectors, value_vectors)
    )
    keys, values, lefts, levels, query = [], [], [], [], {}
    for first in range(0, head_count, group):
        heads = tuple(range(first, first + group))
        extra = 0 if first + group == head_count else None
        results = pl.pallas_call(
            lambda *refs, heads=heads, extra=extra: totals_kernel(heads, extra, *refs),
            in_specs=[HBM] * (2 if extra is None else 3),
            out_specs=[VMEM] * (4 if extra is None else 5),
            out_shape=[
                shape((group, token_count, width), jnp.bfloat16),
                shape((group, token_count, width), jnp.bfloat16),
                shape((group, block_count, width, width), jnp.bfloat16),
                shape((group, width, width), jnp.float32),
            ]
            + ([] if extra is None else [whole]),
            scratch_shapes=[pltpu.SemaphoreType.DMA((group * PIECES * 2 + 1,))],
            compiler_params=params,
            cost_estimate=pl.CostEstimate(flops=0, transcendentals=0, bytes_accessed=6 * MIB),
            name="totals",
        )(key_vectors, value_vectors, *(() if extra is None else (queries,)))
        keys.append(results[0])
        values.append(results[1])
        lefts.append(results[2])
        levels.append(remote_states(results[3], lax.axis_size("ctx")))
        if extra is not None:
            query[extra] = results[4]

    weights, short = pl.pallas_call(
        weights_kernel,
        in_specs=[VMEM, VMEM, ANY],
        out_specs=[VMEM, VMEM],
        out_shape=[shape((token_count, LANES), jnp.float32), shape((token_count, LANES), jnp.bfloat16)],
        compiler_params=params,
        name="weights",
    )(token_rows[None, :], jnp.transpose(weight_table, (2, 1, 0)), lefts[-1])

    parts = []
    for head in range(head_count):
        follow = head + 1 if head + 1 < head_count else None
        place = head % group
        results = pl.pallas_call(
            lambda *refs, head=head, place=place, follow=follow: local_kernel(head, place, follow, *refs),
            in_specs=[VMEM] * 6 + ([] if follow is None else [HBM]),
            out_specs=[VMEM] * (1 if follow is None else 2),
            out_shape=[shape((token_count, width), jnp.float32)] + ([] if follow is None else [whole]),
            scratch_shapes=[] if follow is None else [pltpu.SemaphoreType.DMA(())],
            compiler_params=params,
            cost_estimate=pl.CostEstimate(flops=0, transcendentals=0, bytes_accessed=8 * MIB),
            name="local",
        )(
            query[head], keys[head // group], values[head // group], lefts[head // group], weights, short,
            *(() if follow is None else (queries,)),
        )
        parts.append(results[0])
        if follow is not None:
            query[follow] = results[1]

    out = None
    for first in range(0, head_count, group):
        heads = tuple(range(first, first + group))
        arrived = levels[first // group]
        counts = tuple(len(arrays) for arrays in arrived)
        arrays = [array for arrays in arrived for array in arrays]
        operands = [short] + [query[head] for head in heads] + [parts[head] for head in heads] + arrays
        out = pl.pallas_call(
            lambda *refs, heads=heads, counts=counts: remote_kernel(heads, counts, local_bits, False, *refs),
            in_specs=[VMEM] * len(operands) + ([] if out is None else [HBM]),
            out_specs=HBM,
            out_shape=shape(queries.shape, queries.dtype),
            input_output_aliases={} if out is None else {len(operands): 0},
            scratch_shapes=[
                pltpu.VMEM((group, token_count, width), jnp.bfloat16),
                pltpu.SemaphoreType.DMA((group * PIECES,)),
            ],
            compiler_params=params,
            cost_estimate=pl.CostEstimate(flops=0, transcendentals=0, bytes_accessed=4 * MIB),
            name="remote",
        )(*operands, *(() if out is None else (out,)))
    return out


def solution(mesh):
    placed = (
        P(("groups", "ctx"), "head"),
        P(("groups", "ctx"), "head"),
        P(("groups", "ctx"), "head"),
        P(("groups", "ctx")),
        P(None, "head", None),
    )
    return jax.shard_map(
        body, mesh=mesh, in_specs=placed, out_specs=P(("groups", "ctx"), "head"), check_vma=False
    )
```

```python
import jax
import jax.numpy as jnp
from jax import lax
from jax.experimental import pallas as pl
from jax.experimental.pallas import tpu as pltpu
from jax.sharding import PartitionSpec as P

BLOCK = 256
HALF = BLOCK // 2
BLOCK_BITS = BLOCK.bit_length() - 1
ROWS = 8
ROW_BITS = ROWS.bit_length() - 1
TILES = HALF // ROWS
LANES = 128
SLOT = 32
PIECES = 4
FLIGHT = 2
MIB = 1 << 20
VMEM = pl.BlockSpec(memory_space=pltpu.VMEM)
HBM = pl.BlockSpec(memory_space=pltpu.HBM)
ROW_BY_ROW = (((1,), (1,)), ((), ()))


def columns(head):
    return pl.ds(head * LANES, LANES)


def level_weights(rows_ref, table_ref, weight_ref, local_bits):
    levels, heads, table_rows = table_ref.shape
    device = lax.axis_index("ctx")
    level = lax.broadcasted_iota(jnp.int32, (levels, table_rows), 0)
    scale = jnp.ones((levels, table_rows), jnp.float32)
    for level_id in range(2, levels):
        scale = jnp.where(level == level_id, 2.0 ** (-(level_id - 1) / 2), scale)
    for bit in range(lax.axis_size("ctx").bit_length() - 1):
        held = (device >> bit & 1).astype(jnp.float32)
        scale = jnp.where(level == local_bits + 1 + bit, scale * held, scale)
    slots = []
    for head in range(heads):
        slots.append(table_ref[:, head, :] * scale)
        slots.append(jnp.zeros((SLOT - levels, table_rows), jnp.float32))
    table = jnp.concatenate(slots, axis=0)
    high = table.astype(jnp.bfloat16)
    low = (table - high.astype(jnp.float32)).astype(jnp.bfloat16)
    ids = lax.broadcasted_iota(jnp.int32, (table_rows, BLOCK), 0)
    for start in range(0, weight_ref.shape[1], BLOCK):
        pick = (ids == rows_ref[:, start : start + BLOCK]).astype(jnp.float32).astype(jnp.bfloat16)
        weight_ref[:, start : start + BLOCK] = jnp.dot(
            high, pick, preferred_element_type=jnp.float32
        ) + jnp.dot(low, pick, preferred_element_type=jnp.float32)


def totals_kernel(heads, with_weights, follow, local_bits, *refs):
    refs = list(refs)
    key_hbm, value_hbm = refs.pop(0), refs.pop(0)
    small = [refs.pop(0), refs.pop(0)] if with_weights else []
    query_hbm = refs.pop(0) if follow is not None else None
    key_ref, turned_ref, left_ref, total_ref = (refs.pop(0) for _ in range(4))
    weight_ref = refs.pop(0) if with_weights else None
    query_ref = refs.pop(0) if follow is not None else None
    value_ref, sems = refs.pop(0), refs.pop(0)
    count = len(heads)
    token_count = key_ref.shape[1]
    block_count = token_count // BLOCK
    size = token_count // PIECES
    blocks = block_count // PIECES

    copies = []
    for place, head in enumerate(heads):
        for piece in range(PIECES):
            rows = pl.ds(piece * size, size)
            copies.append([
                pltpu.make_async_copy(
                    source.at[rows, columns(head)], target.at[place, rows, :], sems.at[len(copies), which]
                )
                for which, (source, target) in enumerate(((key_hbm, key_ref), (value_hbm, value_ref)))
            ])
    if with_weights:
        staged = [
            pltpu.make_async_copy(source, target, sems.at[len(copies), which])
            for which, (source, target) in enumerate(zip(small, refs))
        ]
        for copy in staged:
            copy.start()
    for step in range(FLIGHT):
        for copy in copies[step]:
            copy.start()
    if with_weights:
        for copy in staged:
            copy.wait()
        level_weights(refs[0], refs[1], weight_ref, local_bits)
    for step, pair in enumerate(copies):
        for copy in pair:
            copy.wait()
        if step + FLIGHT < len(copies):
            for copy in copies[step + FLIGHT]:
                copy.start()
        elif follow is not None and step + FLIGHT == len(copies):
            ahead = pltpu.make_async_copy(
                query_hbm.at[:, columns(follow)], query_ref, sems.at[len(copies), 0]
            )
            ahead.start()
        place, piece = divmod(step, PIECES)
        if piece == 0:
            held = {}
        for block in range(piece * blocks, (piece + 1) * blocks):
            rows = slice(block * BLOCK, (block + 1) * BLOCK)
            turned = jnp.transpose(value_ref[place, rows, :])
            turned_ref[place, :, rows] = turned
            carry = jnp.dot(turned, key_ref[place, rows, :], preferred_element_type=jnp.float32)
            bit = 0
            while block >> bit & 1:
                carry = carry + held.pop(bit)
                bit += 1
            held[bit] = carry
            if block + 1 < block_count:
                left_ref[place, block] = carry.astype(jnp.bfloat16)
            else:
                total_ref[place] = carry
    if follow is not None:
        ahead.wait()


def local_kernel(head, place, follow, *refs):
    query_ref, key_ref, turned_ref, left_ref, weight_ref = refs[:5]
    refs = list(refs[5:])
    query_hbm = refs.pop(0) if follow is not None else None
    part_ref = refs.pop(0)
    if follow is not None:
        next_ref = refs.pop(0)
        ahead = pltpu.make_async_copy(query_hbm.at[:, columns(follow)], next_ref, refs.pop(0))
        ahead.start()
    tile_ref = refs.pop(0)
    token_count = query_ref.shape[0]
    block_count = token_count // BLOCK
    base = head * SLOT

    lane = lax.broadcasted_iota(jnp.int32, (ROWS, HALF), 1)
    source = lax.broadcasted_iota(jnp.int32, (ROWS, HALF), 0)
    lane_tile = lane >> ROW_BITS
    near = (lane & ROWS - 1) ^ source
    behind = source > (lane & ROWS - 1)
    far_tile = lax.broadcasted_iota(jnp.int32, (TILES, HALF), 1) >> ROW_BITS
    far_source = lax.broadcasted_iota(jnp.int32, (TILES, HALF), 0)
    far = far_tile ^ far_source
    far_behind = far_source > far_tile

    def level_row(level, first, count):
        return weight_ref[base + level : base + level + 1, first : first + count]

    def own_half(scores, first, slot):
        chosen = jnp.broadcast_to(level_row(0, first, HALF), (ROWS, HALF))
        for bit in range(ROW_BITS):
            chosen = jnp.where(near >= 2**bit, level_row(1 + bit, first, HALF), chosen)
        chosen = jnp.where(behind, 0.0, chosen)
        spread = jnp.zeros((TILES, HALF), jnp.float32)
        for bit in range(BLOCK_BITS - 1 - ROW_BITS):
            spread = jnp.where(far >= 2**bit, level_row(1 + ROW_BITS + bit, first, HALF), spread)
        tile_ref[slot] = jnp.where(far_behind, 0.0, spread)
        rows = []
        for tile in range(TILES):
            weights = jnp.where(lane_tile == tile, chosen, tile_ref[slot, tile : tile + 1, :])
            rows.append(scores[tile * ROWS : (tile + 1) * ROWS] * weights)
        return jnp.concatenate(rows, axis=0).astype(jnp.bfloat16)

    for block in range(block_count):
        start = block * BLOCK
        rows = slice(start, start + BLOCK)
        bits = [bit for bit in range(block_count.bit_length() - 1) if block >> bit & 1]
        stacked = [key_ref[place, rows, :]] + [left_ref[place, (block >> bit << bit) - 1] for bit in bits]
        scores = lax.dot_general(
            jnp.concatenate(stacked, axis=0), query_ref[rows, :], ROW_BY_ROW,
            preferred_element_type=jnp.float32,
        )
        low = own_half(scores[:HALF, :HALF], start, 2 * block)
        high = own_half(scores[HALF:BLOCK, HALF:], start + HALF, 2 * block + 1)
        across = (scores[:HALF, HALF:] * level_row(BLOCK_BITS, start + HALF, HALF)).astype(jnp.bfloat16)
        weighted = jnp.concatenate(
            [
                jnp.concatenate([low, across], axis=1),
                jnp.concatenate([jnp.zeros_like(low), high], axis=1),
            ],
            axis=0,
        )
        result = jnp.dot(turned_ref[place, :, rows], weighted, preferred_element_type=jnp.float32)
        for spot, bit in enumerate(bits):
            first = BLOCK + spot * LANES
            result = result + scores[first : first + LANES] * level_row(BLOCK_BITS + 1 + bit, start, BLOCK)
        part_ref[:, rows] = result
    if follow is not None:
        ahead.wait()


def remote_kernel(heads, local_bits, bit_count, *refs):
    count = len(heads)
    weight_ref = refs[0]
    query_refs = refs[1 : 1 + count]
    part_refs = refs[1 + count : 1 + 2 * count]
    state_refs = refs[1 + 2 * count : 1 + 2 * count + bit_count]
    out_hbm, buffer, sems = refs[-3:]
    token_count = weight_ref.shape[1]
    size = token_count // PIECES
    copies = []
    for place, head in enumerate(heads):
        states = jnp.concatenate([ref[place] for ref in state_refs], axis=0).astype(jnp.bfloat16)
        for start in range(0, token_count, BLOCK):
            rows = slice(start, start + BLOCK)
            product = lax.dot_general(
                states, query_refs[place][rows, :], ROW_BY_ROW, preferred_element_type=jnp.float32
            )
            result = part_refs[place][:, rows]
            for bit in range(bit_count):
                row = head * SLOT + local_bits + 1 + bit
                result = result + product[bit * LANES : (bit + 1) * LANES] * weight_ref[row : row + 1, rows]
            buffer[place, rows, :] = jnp.transpose(result.astype(buffer.dtype))
            if (start + BLOCK) % size == 0:
                piece = pl.ds(start + BLOCK - size, size)
                copies.append(
                    pltpu.make_async_copy(
                        buffer.at[place, piece, :], out_hbm.at[piece, columns(head)], sems.at[len(copies)]
                    )
                )
                copies[-1].start()
    for copy in copies:
        copy.wait()


def join_kernel(left_ref, right_ref, out_ref):
    out_ref[...] = left_ref[...] + right_ref[...]


def sibling_totals(total, device_count):
    received = []
    for bit in range(device_count.bit_length() - 1):
        if bit:
            total = pl.pallas_call(
                join_kernel,
                in_specs=[VMEM, VMEM],
                out_specs=VMEM,
                out_shape=jax.ShapeDtypeStruct(total.shape, total.dtype),
                compiler_params=pltpu.CompilerParams(vmem_limit_bytes=2 * MIB),
                name="join",
            )(total, received[-1])
        pairs = [(device, device ^ 2**bit) for device in range(device_count)]
        received.append(lax.ppermute(total, "ctx", pairs))
    return received


def body(queries, key_vectors, value_vectors, token_rows, weight_table):
    table_rows, head_count, level_count = weight_table.shape
    token_count = queries.shape[0]
    width = queries.shape[1] // head_count
    block_count = token_count // BLOCK
    local_bits = token_count.bit_length() - 1
    bit_count = lax.axis_size("ctx").bit_length() - 1
    group = head_count // 2
    shape = jax.ShapeDtypeStruct
    whole = shape((token_count, width), jnp.bfloat16)
    params = pltpu.CompilerParams(vmem_limit_bytes=8 * MIB)
    in_hbm = lambda array: pltpu.with_memory_space_constraint(array, pltpu.HBM)
    queries, key_vectors, value_vectors = in_hbm(queries), in_hbm(key_vectors), in_hbm(value_vectors)
    small = (in_hbm(token_rows[None, :]), in_hbm(jnp.transpose(weight_table, (2, 1, 0))))

    keys, turned, lefts, received, query = [], [], [], [], {}
    for first in range(0, head_count, group):
        heads = tuple(range(first, first + group))
        with_weights = first == 0
        follow = 0 if first + group == head_count else None
        operands = [key_vectors, value_vectors]
        shapes = [
            shape((group, token_count, width), jnp.bfloat16),
            shape((group, width, token_count), jnp.bfloat16),
            shape((group, block_count, width, width), jnp.bfloat16),
            shape((group, width, width), jnp.float32),
        ]
        scratch = [
            pltpu.VMEM((group, token_count, width), jnp.bfloat16),
            pltpu.SemaphoreType.DMA((group * PIECES + 1, 2)),
        ]
        if with_weights:
            operands += small
            shapes.append(shape((head_count * SLOT, token_count), jnp.float32))
            scratch += [
                pltpu.VMEM((1, token_count), jnp.int32),
                pltpu.VMEM((level_count, head_count, table_rows), jnp.float32),
            ]
        if follow is not None:
            operands.append(queries)
            shapes.append(whole)
        results = pl.pallas_call(
            lambda *refs, args=(heads, with_weights, follow, local_bits): totals_kernel(*args, *refs),
            in_specs=[HBM] * len(operands),
            out_specs=[VMEM] * len(shapes),
            out_shape=shapes,
            scratch_shapes=scratch,
            compiler_params=params,
            name="totals",
        )(*operands)
        keys.append(results[0])
        turned.append(results[1])
        lefts.append(results[2])
        received.append(sibling_totals(results[3], lax.axis_size("ctx")))
        if with_weights:
            weights = results[4]
        if follow is not None:
            query[follow] = results[-1]

    parts = []
    for head in range(head_count):
        follow = head + 1 if head + 1 < head_count else None
        of = head // group
        results = pl.pallas_call(
            lambda *refs, args=(head, head % group, follow): local_kernel(*args, *refs),
            in_specs=[VMEM] * 5 + ([] if follow is None else [HBM]),
            out_specs=[VMEM] * (1 if follow is None else 2),
            out_shape=[shape((width, token_count), jnp.float32)] + ([] if follow is None else [whole]),
            scratch_shapes=([] if follow is None else [pltpu.SemaphoreType.DMA(())])
            + [pltpu.VMEM((2 * block_count, TILES, HALF), jnp.float32)],
            compiler_params=params,
            name="local",
        )(
            query[head], keys[of], turned[of], lefts[of], weights,
            *(() if follow is None else (queries,)),
        )
        parts.append(results[0])
        if follow is not None:
            query[follow] = results[1]

    out = None
    for first in range(0, head_count, group):
        heads = tuple(range(first, first + group))
        operands = [weights] + [query[head] for head in heads] + [parts[head] for head in heads]
        operands += received[first // group]
        out = pl.pallas_call(
            lambda *refs, heads=heads: remote_kernel(heads, local_bits, bit_count, *refs),
            in_specs=[VMEM] * len(operands) + ([] if out is None else [HBM]),
            out_specs=HBM,
            out_shape=shape(queries.shape, queries.dtype),
            input_output_aliases={} if out is None else {len(operands): 0},
            scratch_shapes=[
                pltpu.VMEM((group, token_count, width), jnp.bfloat16),
                pltpu.SemaphoreType.DMA((group * PIECES,)),
            ],
            compiler_params=params,
            name="remote",
        )(*operands, *(() if out is None else (out,)))
    return out


def solution(mesh):
    placed = (
        P(("groups", "ctx"), "head"),
        P(("groups", "ctx"), "head"),
        P(("groups", "ctx"), "head"),
        P(("groups", "ctx")),
        P(None, "head", None),
    )
    return jax.shard_map(
        body, mesh=mesh, in_specs=placed, out_specs=P(("groups", "ctx"), "head"), check_vma=False
    )
```

```python
import jax
import jax.numpy as jnp
from jax import lax
from jax.experimental import pallas as pl
from jax.experimental.pallas import tpu as pltpu
from jax.sharding import PartitionSpec as P

BLOCK = 256
HALF = BLOCK // 2
BLOCK_BITS = BLOCK.bit_length() - 1
ROWS = 8
ROW_BITS = ROWS.bit_length() - 1
TILES = HALF // ROWS
LANES = 128
SLOT = 32
PIECES = 8
GROUPS = 2
MIB = 1 << 20
VMEM = pl.BlockSpec(memory_space=pltpu.VMEM)
HBM = pl.BlockSpec(memory_space=pltpu.HBM)
ROW_BY_ROW = (((1,), (1,)), ((), ()))


def level_weights(rows_ref, table_ref, weight_ref, local_bits):
    levels, heads, table_rows = table_ref.shape
    device = lax.axis_index("ctx")
    level = lax.broadcasted_iota(jnp.int32, (levels, table_rows), 0)
    scale = jnp.ones((levels, table_rows), jnp.float32)
    for level_id in range(2, levels):
        scale = jnp.where(level == level_id, 2.0 ** (-(level_id - 1) / 2), scale)
    for bit in range(lax.axis_size("ctx").bit_length() - 1):
        held = (device >> bit & 1).astype(jnp.float32)
        scale = jnp.where(level == local_bits + 1 + bit, scale * held, scale)
    slots = []
    for head in range(heads):
        slots.append(table_ref[:, head, :] * scale)
        slots.append(jnp.zeros((SLOT - levels, table_rows), jnp.float32))
    table = jnp.concatenate(slots, axis=0)
    high = table.astype(jnp.bfloat16)
    low = (table - high.astype(jnp.float32)).astype(jnp.bfloat16)
    ids = lax.broadcasted_iota(jnp.int32, (table_rows, BLOCK), 0)
    for start in range(0, weight_ref.shape[1], BLOCK):
        pick = (ids == rows_ref[:, start : start + BLOCK]).astype(jnp.float32).astype(jnp.bfloat16)
        weight_ref[:, start : start + BLOCK] = jnp.dot(
            high, pick, preferred_element_type=jnp.float32
        ) + jnp.dot(low, pick, preferred_element_type=jnp.float32)


def pipelined(units, begin, finish):
    ahead = begin(units[0])
    for unit, following in zip(units, units[1:] + [None]):
        held, ahead = ahead, None if following is None else begin(following)
        finish(unit, held)


def totals_kernel(local_bits, key_hbm, value_hbm, rows_hbm, table_hbm, key_ref, turned_ref, left_ref, *refs):
    total_refs = refs[:GROUPS]
    weight_ref, value_ref, rows_ref, table_ref, sems, small_sems = refs[GROUPS:]
    token_count = key_ref.shape[0]
    head_count = turned_ref.shape[0]
    group = head_count // GROUPS
    block_count = token_count // BLOCK
    size = token_count // PIECES
    blocks = block_count // PIECES
    staged = [
        pltpu.make_async_copy(source, target, small_sems.at[which])
        for which, (source, target) in enumerate(((rows_hbm, rows_ref), (table_hbm, table_ref)))
    ]
    copies = []
    for piece in range(PIECES):
        rows = pl.ds(piece * size, size)
        copies.append([
            pltpu.make_async_copy(source.at[rows, :], target.at[rows, :], sems.at[piece, which])
            for which, (source, target) in enumerate(((key_hbm, key_ref), (value_hbm, value_ref)))
        ])
    for copy in staged + [copy for pair in copies for copy in pair]:
        copy.start()
    for copy in staged:
        copy.wait()
    level_weights(rows_ref, table_ref, weight_ref, local_bits)

    held = [{} for _ in range(head_count)]

    def begin(unit):
        block, head = unit
        rows = slice(block * BLOCK, (block + 1) * BLOCK)
        turned = jnp.transpose(value_ref[rows, head * LANES : (head + 1) * LANES])
        turned_ref[head, :, rows] = turned
        return turned

    def finish(unit, turned):
        block, head = unit
        rows = slice(block * BLOCK, (block + 1) * BLOCK)
        carry = jnp.dot(
            turned, key_ref[rows, head * LANES : (head + 1) * LANES], preferred_element_type=jnp.float32
        )
        bit = 0
        while block >> bit & 1:
            carry = carry + held[head].pop(bit)
            bit += 1
        held[head][bit] = carry
        if block + 1 < block_count:
            left_ref[head, block] = carry.astype(jnp.bfloat16)
        else:
            total_refs[head // group][head % group] = carry

    for piece, pair in enumerate(copies):
        for copy in pair:
            copy.wait()
        span = range(piece * blocks, (piece + 1) * blocks)
        pipelined([(block, head) for block in span for head in range(head_count)], begin, finish)


def local_kernel(head, loads, *refs):
    query_in, key_ref, turned_ref, left_ref, weight_ref, part_ref = refs[:6]
    refs = list(refs[6:])
    query_ref = refs.pop(0) if loads else query_in
    tile_ref = refs.pop(0)
    token_count = query_ref.shape[0]
    block_count = token_count // BLOCK
    columns = slice(head * LANES, (head + 1) * LANES)
    base = head * SLOT
    if loads:
        sems = refs.pop(0)
        size = token_count // PIECES
        copies = []
        for piece in range(PIECES):
            rows = pl.ds(piece * size, size)
            copies.append(pltpu.make_async_copy(query_in.at[rows, :], query_ref.at[rows, :], sems.at[piece]))
            copies[-1].start()

    lane = lax.broadcasted_iota(jnp.int32, (ROWS, HALF), 1)
    source = lax.broadcasted_iota(jnp.int32, (ROWS, HALF), 0)
    lane_tile = lane >> ROW_BITS
    near = (lane & ROWS - 1) ^ source
    behind = source > (lane & ROWS - 1)
    far_tile = lax.broadcasted_iota(jnp.int32, (TILES, HALF), 1) >> ROW_BITS
    far_source = lax.broadcasted_iota(jnp.int32, (TILES, HALF), 0)
    far = far_tile ^ far_source
    far_behind = far_source > far_tile

    def level_row(level, first, count):
        return weight_ref[base + level : base + level + 1, first : first + count]

    def own_half(scores, first, slot):
        chosen = jnp.broadcast_to(level_row(0, first, HALF), (ROWS, HALF))
        for bit in range(ROW_BITS):
            chosen = jnp.where(near >= 2**bit, level_row(1 + bit, first, HALF), chosen)
        chosen = jnp.where(behind, 0.0, chosen)
        spread = jnp.zeros((TILES, HALF), jnp.float32)
        for bit in range(BLOCK_BITS - 1 - ROW_BITS):
            spread = jnp.where(far >= 2**bit, level_row(1 + ROW_BITS + bit, first, HALF), spread)
        tile_ref[slot] = jnp.where(far_behind, 0.0, spread)
        rows = []
        for tile in range(TILES):
            weights = jnp.where(lane_tile == tile, chosen, tile_ref[slot, tile : tile + 1, :])
            rows.append(scores[tile * ROWS : (tile + 1) * ROWS] * weights)
        return jnp.concatenate(rows, axis=0).astype(jnp.bfloat16)

    def begin(block):
        rows = slice(block * BLOCK, (block + 1) * BLOCK)
        if loads and block % (block_count // PIECES) == 0:
            copies[block // (block_count // PIECES)].wait()
        query = jnp.transpose(query_ref[rows, columns])
        return query, jnp.dot(key_ref[rows, columns], query, preferred_element_type=jnp.float32)

    def finish(block, begun):
        query, scores = begun
        start = block * BLOCK
        rows = slice(start, start + BLOCK)
        low = own_half(scores[:HALF, :HALF], start, 2 * block)
        high = own_half(scores[HALF:, HALF:], start + HALF, 2 * block + 1)
        across = (scores[:HALF, HALF:] * level_row(BLOCK_BITS, start + HALF, HALF)).astype(jnp.bfloat16)
        right = [
            jnp.concatenate([low, across], axis=1),
            jnp.concatenate([jnp.zeros_like(low), high], axis=1),
        ]
        left = [turned_ref[head, :, rows]]
        for bit in range(block_count.bit_length() - 1):
            if block >> bit & 1:
                scaled = query.astype(jnp.float32) * level_row(BLOCK_BITS + 1 + bit, start, BLOCK)
                right.append(scaled.astype(jnp.bfloat16))
                left.append(left_ref[head, (block >> bit << bit) - 1])
        part_ref[:, rows] = jnp.dot(
            jnp.concatenate(left, axis=1), jnp.concatenate(right, axis=0),
            preferred_element_type=jnp.float32,
        )

    pipelined(list(range(block_count)), begin, finish)


def remote_kernel(heads, local_bits, bit_count, *refs):
    count = len(heads)
    weight_ref, query_ref = refs[:2]
    part_refs = refs[2 : 2 + count]
    state_refs = refs[2 + count : 2 + count + bit_count]
    out_hbm, buffer, sems = refs[-3:]
    token_count = weight_ref.shape[1]
    size = token_count // PIECES
    states = [
        jnp.concatenate([ref[place] for ref in state_refs], axis=0).astype(jnp.bfloat16)
        for place in range(count)
    ]
    copies = []

    def begin(unit):
        start, place = unit
        columns = slice(heads[place] * LANES, (heads[place] + 1) * LANES)
        return lax.dot_general(
            states[place], query_ref[start : start + BLOCK, columns], ROW_BY_ROW,
            preferred_element_type=jnp.float32,
        )

    def finish(unit, product):
        start, place = unit
        rows = slice(start, start + BLOCK)
        result = part_refs[place][:, rows]
        for bit in range(bit_count):
            row = heads[place] * SLOT + local_bits + 1 + bit
            result = result + product[bit * LANES : (bit + 1) * LANES] * weight_ref[row : row + 1, rows]
        buffer[rows, place * LANES : (place + 1) * LANES] = jnp.transpose(result.astype(buffer.dtype))
        if place + 1 == count and (start + BLOCK) % size == 0:
            piece = pl.ds(start + BLOCK - size, size)
            target = out_hbm.at[piece, pl.ds(heads[0] * LANES, count * LANES)]
            copies.append(pltpu.make_async_copy(buffer.at[piece, :], target, sems.at[len(copies)]))
            copies[-1].start()

    units = [(start, place) for start in range(0, token_count, BLOCK) for place in range(count)]
    pipelined(units, begin, finish)
    for copy in copies:
        copy.wait()


def join_kernel(left_ref, right_ref, after_ref, out_ref):
    out_ref[...] = left_ref[...] + right_ref[...]


def sibling_totals(total, device_count, after):
    received = []
    for bit in range(device_count.bit_length() - 1):
        if bit:
            total = pl.pallas_call(
                join_kernel,
                in_specs=[VMEM, VMEM, pl.BlockSpec(memory_space=pl.ANY)],
                out_specs=VMEM,
                out_shape=jax.ShapeDtypeStruct(total.shape, total.dtype),
                compiler_params=pltpu.CompilerParams(vmem_limit_bytes=2 * MIB),
                name="join",
            )(total, received[-1], after)
        pairs = [(device, device ^ 2**bit) for device in range(device_count)]
        received.append(lax.ppermute(total, "ctx", pairs))
    return received


def body(queries, key_vectors, value_vectors, token_rows, weight_table):
    table_rows, head_count, level_count = weight_table.shape
    token_count = queries.shape[0]
    width = queries.shape[1] // head_count
    block_count = token_count // BLOCK
    local_bits = token_count.bit_length() - 1
    devices = lax.axis_size("ctx")
    bit_count = devices.bit_length() - 1
    group = head_count // GROUPS
    shape = jax.ShapeDtypeStruct
    whole = shape(queries.shape, queries.dtype)
    params = pltpu.CompilerParams(vmem_limit_bytes=8 * MIB)
    in_hbm = lambda array: pltpu.with_memory_space_constraint(array, pltpu.HBM)
    queries, key_vectors, value_vectors = in_hbm(queries), in_hbm(key_vectors), in_hbm(value_vectors)

    keys, turned, lefts, *totals, weights = pl.pallas_call(
        lambda *refs: totals_kernel(local_bits, *refs),
        in_specs=[HBM] * 4,
        out_specs=[VMEM] * (4 + GROUPS),
        out_shape=[
            whole,
            shape((head_count, width, token_count), jnp.bfloat16),
            shape((head_count, block_count, width, width), jnp.bfloat16),
            *[shape((group, width, width), jnp.float32)] * GROUPS,
            shape((head_count * SLOT, token_count), jnp.float32),
        ],
        scratch_shapes=[
            pltpu.VMEM(queries.shape, queries.dtype),
            pltpu.VMEM((1, token_count), jnp.int32),
            pltpu.VMEM((level_count, head_count, table_rows), jnp.float32),
            pltpu.SemaphoreType.DMA((PIECES, 2)),
            pltpu.SemaphoreType.DMA((2,)),
        ],
        compiler_params=params,
        name="totals",
    )(key_vectors, value_vectors, in_hbm(token_rows[None, :]), in_hbm(jnp.transpose(weight_table, (2, 1, 0))))

    parts = []
    query = queries
    for head in range(head_count):
        loads = head == 0
        results = pl.pallas_call(
            lambda *refs, head=head, loads=loads: local_kernel(head, loads, *refs),
            in_specs=[HBM if loads else VMEM] + [VMEM] * 4,
            out_specs=[VMEM] * (2 if loads else 1),
            out_shape=[shape((width, token_count), jnp.float32)] + ([whole] if loads else []),
            scratch_shapes=[pltpu.VMEM((2 * block_count, TILES, HALF), jnp.float32)]
            + ([pltpu.SemaphoreType.DMA((PIECES,))] if loads else []),
            compiler_params=params,
            name="local",
        )(query, keys, turned, lefts, weights)
        parts.append(results[0])
        if loads:
            query = results[1]

    received = [sibling_totals(total, devices, parts[0]) for total in totals]
    out = None
    for first in range(0, head_count, group):
        heads = tuple(range(first, first + group))
        operands = [weights, query] + [parts[head] for head in heads] + received[first // group]
        out = pl.pallas_call(
            lambda *refs, heads=heads: remote_kernel(heads, local_bits, bit_count, *refs),
            in_specs=[VMEM] * len(operands) + ([] if out is None else [HBM]),
            out_specs=HBM,
            out_shape=whole,
            input_output_aliases={} if out is None else {len(operands): 0},
            scratch_shapes=[
                pltpu.VMEM((token_count, group * width), jnp.bfloat16),
                pltpu.SemaphoreType.DMA((PIECES,)),
            ],
            compiler_params=params,
            name="remote",
        )(*operands, *(() if out is None else (out,)))
    return out


def solution(mesh):
    placed = (
        P(("groups", "ctx"), "head"),
        P(("groups", "ctx"), "head"),
        P(("groups", "ctx"), "head"),
        P(("groups", "ctx")),
        P(None, "head", None),
    )
    return jax.shard_map(
        body, mesh=mesh, in_specs=placed, out_specs=P(("groups", "ctx"), "head"), check_vma=False
    )
```

```python
import jax
import jax.numpy as jnp
from jax import lax
from jax.experimental import pallas as pl
from jax.experimental.pallas import tpu as pltpu
from jax.sharding import PartitionSpec as P

BLOCK = 256
HALF = BLOCK // 2
BLOCK_BITS = BLOCK.bit_length() - 1
ROWS = 8
ROW_BITS = ROWS.bit_length() - 1
TILES = HALF // ROWS
LANES = 128
SLOT = 32
PIECES = 8
GROUPS = 2
MIB = 1 << 20
VMEM = pl.BlockSpec(memory_space=pltpu.VMEM)
HBM = pl.BlockSpec(memory_space=pltpu.HBM)
ANY = pl.BlockSpec(memory_space=pl.ANY)
ROW_BY_ROW = (((1,), (1,)), ((), ()))


def level_weights(rows_ref, table_ref, weight_ref, local_bits):
    levels, heads, table_rows = table_ref.shape
    device = lax.axis_index("ctx")
    level = lax.broadcasted_iota(jnp.int32, (levels, table_rows), 0)
    scale = jnp.ones((levels, table_rows), jnp.float32)
    for level_id in range(2, levels):
        scale = jnp.where(level == level_id, 2.0 ** (-(level_id - 1) / 2), scale)
    for bit in range(lax.axis_size("ctx").bit_length() - 1):
        held = (device >> bit & 1).astype(jnp.float32)
        scale = jnp.where(level == local_bits + 1 + bit, scale * held, scale)
    slots = []
    for head in range(heads):
        slots.append(table_ref[:, head, :] * scale)
        slots.append(jnp.zeros((SLOT - levels, table_rows), jnp.float32))
    table = jnp.concatenate(slots, axis=0)
    high = table.astype(jnp.bfloat16)
    low = (table - high.astype(jnp.float32)).astype(jnp.bfloat16)
    ids = lax.broadcasted_iota(jnp.int32, (table_rows, BLOCK), 0)
    for start in range(0, weight_ref.shape[1], BLOCK):
        pick = (ids == rows_ref[:, start : start + BLOCK]).astype(jnp.float32).astype(jnp.bfloat16)
        weight_ref[:, start : start + BLOCK] = jnp.dot(
            high, pick, preferred_element_type=jnp.float32
        ) + jnp.dot(low, pick, preferred_element_type=jnp.float32)


def pipelined(units, begin, finish):
    ahead = begin(units[0])
    for unit, following in zip(units, units[1:] + [None]):
        held, ahead = ahead, None if following is None else begin(following)
        finish(unit, held)


def totals_kernel(key_hbm, value_hbm, key_ref, turned_ref, left_ref, *refs):
    total_refs = refs[:GROUPS]
    value_ref, sems = refs[GROUPS:]
    token_count = key_ref.shape[0]
    head_count = turned_ref.shape[0]
    group = head_count // GROUPS
    block_count = token_count // BLOCK
    size = token_count // PIECES
    blocks = block_count // PIECES
    copies = []
    for piece in range(PIECES):
        rows = pl.ds(piece * size, size)
        copies.append([
            pltpu.make_async_copy(source.at[rows, :], target.at[rows, :], sems.at[piece, which])
            for which, (source, target) in enumerate(((key_hbm, key_ref), (value_hbm, value_ref)))
        ])
    for pair in copies:
        for copy in pair:
            copy.start()

    held = [{} for _ in range(head_count)]

    def begin(unit):
        block, head = unit
        rows = slice(block * BLOCK, (block + 1) * BLOCK)
        turned = jnp.transpose(value_ref[rows, head * LANES : (head + 1) * LANES])
        turned_ref[head, :, rows] = turned
        return turned

    def finish(unit, turned):
        block, head = unit
        rows = slice(block * BLOCK, (block + 1) * BLOCK)
        carry = jnp.dot(
            turned, key_ref[rows, head * LANES : (head + 1) * LANES], preferred_element_type=jnp.float32
        )
        bit = 0
        while block >> bit & 1:
            carry = carry + held[head].pop(bit)
            bit += 1
        held[head][bit] = carry
        if block + 1 < block_count:
            left_ref[head, block] = carry.astype(jnp.bfloat16)
        else:
            total_refs[head // group][head % group] = carry

    for piece, pair in enumerate(copies):
        for copy in pair:
            copy.wait()
        span = range(piece * blocks, (piece + 1) * blocks)
        pipelined([(block, head) for block in span for head in range(head_count)], begin, finish)


def prepare_kernel(local_bits, after_ref, query_hbm, rows_hbm, table_hbm, weight_ref, query_ref, *refs):
    rows_ref, table_ref, sems = refs
    small = [
        pltpu.make_async_copy(rows_hbm, rows_ref, sems.at[0]),
        pltpu.make_async_copy(table_hbm, table_ref, sems.at[1]),
    ]
    large = pltpu.make_async_copy(query_hbm, query_ref, sems.at[2])
    for copy in small + [large]:
        copy.start()
    for copy in small:
        copy.wait()
    level_weights(rows_ref, table_ref, weight_ref, local_bits)
    large.wait()


def local_kernel(head, place, local_bits, *refs):
    query_ref, key_ref, turned_ref, left_ref, weight_ref = refs[:5]
    state_refs = refs[5:-2]
    part_ref, tile_ref = refs[-2:]
    token_count = query_ref.shape[0]
    block_count = token_count // BLOCK
    columns = slice(head * LANES, (head + 1) * LANES)
    base = head * SLOT
    states = [(local_bits + 1 + bit, ref[place].astype(jnp.bfloat16)) for bit, ref in enumerate(state_refs)]

    lane = lax.broadcasted_iota(jnp.int32, (ROWS, HALF), 1)
    source = lax.broadcasted_iota(jnp.int32, (ROWS, HALF), 0)
    lane_tile = lane >> ROW_BITS
    near = (lane & ROWS - 1) ^ source
    behind = source > (lane & ROWS - 1)
    far_tile = lax.broadcasted_iota(jnp.int32, (TILES, HALF), 1) >> ROW_BITS
    far_source = lax.broadcasted_iota(jnp.int32, (TILES, HALF), 0)
    far = far_tile ^ far_source
    far_behind = far_source > far_tile

    def level_row(level, first, count):
        return weight_ref[base + level : base + level + 1, first : first + count]

    def own_half(scores, first, slot):
        chosen = jnp.broadcast_to(level_row(0, first, HALF), (ROWS, HALF))
        for bit in range(ROW_BITS):
            chosen = jnp.where(near >= 2**bit, level_row(1 + bit, first, HALF), chosen)
        chosen = jnp.where(behind, 0.0, chosen)
        spread = jnp.zeros((TILES, HALF), jnp.float32)
        for bit in range(BLOCK_BITS - 1 - ROW_BITS):
            spread = jnp.where(far >= 2**bit, level_row(1 + ROW_BITS + bit, first, HALF), spread)
        tile_ref[slot] = jnp.where(far_behind, 0.0, spread)
        rows = []
        for tile in range(TILES):
            weights = jnp.where(lane_tile == tile, chosen, tile_ref[slot, tile : tile + 1, :])
            rows.append(scores[tile * ROWS : (tile + 1) * ROWS] * weights)
        return jnp.concatenate(rows, axis=0).astype(jnp.bfloat16)

    def begin(block):
        rows = slice(block * BLOCK, (block + 1) * BLOCK)
        query = jnp.transpose(query_ref[rows, columns])
        return query, jnp.dot(key_ref[rows, columns], query, preferred_element_type=jnp.float32)

    def finish(block, begun):
        query, scores = begun
        start = block * BLOCK
        rows = slice(start, start + BLOCK)
        low = own_half(scores[:HALF, :HALF], start, 2 * block)
        high = own_half(scores[HALF:, HALF:], start + HALF, 2 * block + 1)
        across = (scores[:HALF, HALF:] * level_row(BLOCK_BITS, start + HALF, HALF)).astype(jnp.bfloat16)
        right = [
            jnp.concatenate([low, across], axis=1),
            jnp.concatenate([jnp.zeros_like(low), high], axis=1),
        ]
        left = [turned_ref[head, :, rows]]
        terms = [
            (BLOCK_BITS + 1 + bit, left_ref[head, (block >> bit << bit) - 1])
            for bit in range(block_count.bit_length() - 1)
            if block >> bit & 1
        ]
        for level, sibling in terms + states:
            scaled = query.astype(jnp.float32) * level_row(level, start, BLOCK)
            right.append(scaled.astype(jnp.bfloat16))
            left.append(sibling)
        part_ref[:, rows] = jnp.dot(
            jnp.concatenate(left, axis=1), jnp.concatenate(right, axis=0),
            preferred_element_type=jnp.float32,
        )

    pipelined(list(range(block_count)), begin, finish)


def remote_kernel(heads, level, *refs):
    count = len(heads)
    weight_ref, query_ref = refs[:2]
    part_refs = refs[2 : 2 + count]
    state_ref = refs[2 + count]
    out_hbm, buffer, sems = refs[-3:]
    token_count = weight_ref.shape[1]
    size = token_count // PIECES
    states = [state_ref[place].astype(jnp.bfloat16) for place in range(count)]
    copies = []

    def begin(unit):
        start, place = unit
        columns = slice(heads[place] * LANES, (heads[place] + 1) * LANES)
        return lax.dot_general(
            states[place], query_ref[start : start + BLOCK, columns], ROW_BY_ROW,
            preferred_element_type=jnp.float32,
        )

    def finish(unit, product):
        start, place = unit
        rows = slice(start, start + BLOCK)
        row = heads[place] * SLOT + level
        result = part_refs[place][:, rows] + product * weight_ref[row : row + 1, rows]
        buffer[rows, place * LANES : (place + 1) * LANES] = jnp.transpose(result.astype(buffer.dtype))
        if place + 1 == count and (start + BLOCK) % size == 0:
            piece = pl.ds(start + BLOCK - size, size)
            target = out_hbm.at[piece, pl.ds(heads[0] * LANES, count * LANES)]
            copies.append(pltpu.make_async_copy(buffer.at[piece, :], target, sems.at[len(copies)]))
            copies[-1].start()

    units = [(start, place) for start in range(0, token_count, BLOCK) for place in range(count)]
    pipelined(units, begin, finish)
    for copy in copies:
        copy.wait()


def join_kernel(left_ref, right_ref, after_ref, out_ref):
    out_ref[...] = left_ref[...] + right_ref[...]


def join(total, received, after):
    return pl.pallas_call(
        join_kernel,
        in_specs=[VMEM, VMEM, ANY],
        out_specs=VMEM,
        out_shape=jax.ShapeDtypeStruct(total.shape, total.dtype),
        compiler_params=pltpu.CompilerParams(vmem_limit_bytes=2 * MIB),
        name="join",
    )(total, received, after)


def exchange(total, bit):
    devices = lax.axis_size("ctx")
    return lax.ppermute(total, "ctx", [(device, device ^ 2**bit) for device in range(devices)])


def body(queries, key_vectors, value_vectors, token_rows, weight_table):
    table_rows, head_count, level_count = weight_table.shape
    token_count = queries.shape[0]
    width = queries.shape[1] // head_count
    block_count = token_count // BLOCK
    local_bits = token_count.bit_length() - 1
    devices = lax.axis_size("ctx")
    bit_count = devices.bit_length() - 1
    group = head_count // GROUPS
    shape = jax.ShapeDtypeStruct
    whole = shape(queries.shape, queries.dtype)
    params = pltpu.CompilerParams(vmem_limit_bytes=8 * MIB)
    in_hbm = lambda array: pltpu.with_memory_space_constraint(array, pltpu.HBM)
    queries, key_vectors, value_vectors = in_hbm(queries), in_hbm(key_vectors), in_hbm(value_vectors)

    keys, turned, lefts, *totals = pl.pallas_call(
        totals_kernel,
        in_specs=[HBM] * 2,
        out_specs=[VMEM] * (3 + GROUPS),
        out_shape=[
            whole,
            shape((head_count, width, token_count), jnp.bfloat16),
            shape((head_count, block_count, width, width), jnp.bfloat16),
            *[shape((group, width, width), jnp.float32)] * GROUPS,
        ],
        scratch_shapes=[
            pltpu.VMEM(queries.shape, queries.dtype),
            pltpu.SemaphoreType.DMA((PIECES, 2)),
        ],
        compiler_params=params,
        name="totals",
    )(key_vectors, value_vectors)

    weights, query = pl.pallas_call(
        lambda *refs: prepare_kernel(local_bits, *refs),
        in_specs=[ANY] + [HBM] * 3,
        out_specs=[VMEM] * 2,
        out_shape=[shape((head_count * SLOT, token_count), jnp.float32), whole],
        scratch_shapes=[
            pltpu.VMEM((1, token_count), jnp.int32),
            pltpu.VMEM((level_count, head_count, table_rows), jnp.float32),
            pltpu.SemaphoreType.DMA((3,)),
        ],
        compiler_params=params,
        name="prepare",
    )(lefts, queries, in_hbm(token_rows[None, :]), in_hbm(jnp.transpose(weight_table, (2, 1, 0))))

    received = [[exchange(total, 0)] for total in totals]
    parts = []
    after = weights
    for index, total in enumerate(totals):
        for bit in range(1, bit_count):
            total = join(total, received[index][-1], after)
            received[index].append(exchange(total, bit))
        for head in range(index * group, (index + 1) * group):
            parts += pl.pallas_call(
                lambda *refs, head=head: local_kernel(head, head % group, local_bits, *refs),
                in_specs=[VMEM] * (5 + bit_count - 1),
                out_specs=[VMEM],
                out_shape=[shape((width, token_count), jnp.float32)],
                scratch_shapes=[pltpu.VMEM((2 * block_count, TILES, HALF), jnp.float32)],
                compiler_params=params,
                name="local",
            )(query, keys, turned, lefts, weights, *received[index][:-1])
        after = parts[0]

    out = None
    for index, arrived in enumerate(received):
        heads = tuple(range(index * group, (index + 1) * group))
        operands = [weights, query] + [parts[head] for head in heads] + [arrived[-1]]
        out = pl.pallas_call(
            lambda *refs, heads=heads: remote_kernel(heads, local_bits + bit_count, *refs),
            in_specs=[VMEM] * len(operands) + ([] if out is None else [HBM]),
            out_specs=HBM,
            out_shape=whole,
            input_output_aliases={} if out is None else {len(operands): 0},
            scratch_shapes=[
                pltpu.VMEM((token_count, group * width), jnp.bfloat16),
                pltpu.SemaphoreType.DMA((PIECES,)),
            ],
            compiler_params=params,
            name="remote",
        )(*operands, *(() if out is None else (out,)))
    return out


def solution(mesh):
    placed = (
        P(("groups", "ctx"), "head"),
        P(("groups", "ctx"), "head"),
        P(("groups", "ctx"), "head"),
        P(("groups", "ctx")),
        P(None, "head", None),
    )
    return jax.shard_map(
        body, mesh=mesh, in_specs=placed, out_specs=P(("groups", "ctx"), "head"), check_vma=False
    )
```

```python
import jax
import jax.numpy as jnp
from jax import lax
from jax.experimental import pallas as pl
from jax.experimental.pallas import tpu as pltpu
from jax.sharding import PartitionSpec as P

BLOCK = 256
HALF = BLOCK // 2
BLOCK_BITS = BLOCK.bit_length() - 1
ROWS = 8
ROW_BITS = ROWS.bit_length() - 1
TILES = HALF // ROWS
LANES = 128
SLOT = 32
PIECES = 8
GROUPS = 2
MIB = 1 << 20
VMEM = pl.BlockSpec(memory_space=pltpu.VMEM)
HBM = pl.BlockSpec(memory_space=pltpu.HBM)
ANY = pl.BlockSpec(memory_space=pl.ANY)
ROW_BY_ROW = (((1,), (1,)), ((), ()))


def scaled_table(table_ref, local_bits):
    levels, heads, table_rows = table_ref.shape
    device = lax.axis_index("ctx")
    level = lax.broadcasted_iota(jnp.int32, (levels, table_rows), 0)
    scale = jnp.ones((levels, table_rows), jnp.float32)
    for level_id in range(2, levels):
        scale = jnp.where(level == level_id, 2.0 ** (-(level_id - 1) / 2), scale)
    for bit in range(lax.axis_size("ctx").bit_length() - 1):
        held = (device >> bit & 1).astype(jnp.float32)
        scale = jnp.where(level == local_bits + 1 + bit, scale * held, scale)
    slots = []
    for head in range(heads):
        slots.append(table_ref[:, head, :] * scale)
        slots.append(jnp.zeros((SLOT - levels, table_rows), jnp.float32))
    table = jnp.concatenate(slots, axis=0)
    high = table.astype(jnp.bfloat16)
    return high, (table - high.astype(jnp.float32)).astype(jnp.bfloat16)


def pipelined(units, begin, finish):
    ahead = begin(units[0])
    for unit, following in zip(units, units[1:] + [None]):
        held, ahead = ahead, None if following is None else begin(following)
        finish(unit, held)


def totals_kernel(local_bits, key_hbm, value_hbm, rows_hbm, table_hbm, key_ref, turned_ref, left_ref, weight_ref, *refs):
    total_refs = refs[:GROUPS]
    value_ref, rows_ref, table_ref, sems, small_sems = refs[GROUPS:]
    token_count = key_ref.shape[0]
    head_count = turned_ref.shape[0]
    group = head_count // GROUPS
    block_count = token_count // BLOCK
    size = token_count // PIECES
    blocks = block_count // PIECES
    copies = []
    for piece in range(PIECES):
        rows = pl.ds(piece * size, size)
        copies.append([
            pltpu.make_async_copy(source.at[rows, :], target.at[rows, :], sems.at[piece, which])
            for which, (source, target) in enumerate(((key_hbm, key_ref), (value_hbm, value_ref)))
        ])
    staged = [
        pltpu.make_async_copy(source, target, small_sems.at[which])
        for which, (source, target) in enumerate(((rows_hbm, rows_ref), (table_hbm, table_ref)))
    ]
    for copy in copies[0] + staged + [copy for pair in copies[1:] for copy in pair]:
        copy.start()

    held = [{} for _ in range(head_count)]

    def begin(unit):
        block, head = unit
        rows = slice(block * BLOCK, (block + 1) * BLOCK)
        turned = jnp.transpose(value_ref[rows, head * LANES : (head + 1) * LANES])
        turned_ref[head, :, rows] = turned
        return turned

    def finish(unit, turned):
        block, head = unit
        rows = slice(block * BLOCK, (block + 1) * BLOCK)
        carry = jnp.dot(
            turned, key_ref[rows, head * LANES : (head + 1) * LANES], preferred_element_type=jnp.float32
        )
        bit = 0
        while block >> bit & 1:
            carry = carry + held[head].pop(bit)
            bit += 1
        held[head][bit] = carry
        if block + 1 < block_count:
            left_ref[head, block] = carry.astype(jnp.bfloat16)
        else:
            total_refs[head // group][head % group] = carry

    for piece, pair in enumerate(copies):
        for copy in pair:
            copy.wait()
        if piece == 1:
            for copy in staged:
                copy.wait()
            high, low = scaled_table(table_ref, local_bits)
        if piece >= 1:
            first = 0 if piece == 1 else piece * blocks
            ids = lax.broadcasted_iota(jnp.int32, (high.shape[1], BLOCK), 0)
            for block in range(first, (piece + 1) * blocks):
                tokens = slice(block * BLOCK, (block + 1) * BLOCK)
                pick = (ids == rows_ref[:, tokens]).astype(jnp.float32).astype(jnp.bfloat16)
                weight_ref[:, tokens] = jnp.dot(
                    high, pick, preferred_element_type=jnp.float32
                ) + jnp.dot(low, pick, preferred_element_type=jnp.float32)
        span = range(piece * blocks, (piece + 1) * blocks)
        pipelined([(block, head) for block in span for head in range(head_count)], begin, finish)


def local_kernel(head, place, local_bits, *refs):
    query_ref, key_ref, turned_ref, left_ref, weight_ref = refs[:5]
    state_refs = refs[5:-2]
    part_ref, tile_ref = refs[-2:]
    token_count = query_ref.shape[0]
    block_count = token_count // BLOCK
    columns = slice(head * LANES, (head + 1) * LANES)
    base = head * SLOT
    states = [(local_bits + 1 + bit, ref[place].astype(jnp.bfloat16)) for bit, ref in enumerate(state_refs)]

    lane = lax.broadcasted_iota(jnp.int32, (ROWS, HALF), 1)
    source = lax.broadcasted_iota(jnp.int32, (ROWS, HALF), 0)
    lane_tile = lane >> ROW_BITS
    near = (lane & ROWS - 1) ^ source
    behind = source > (lane & ROWS - 1)
    far_tile = lax.broadcasted_iota(jnp.int32, (TILES, HALF), 1) >> ROW_BITS
    far_source = lax.broadcasted_iota(jnp.int32, (TILES, HALF), 0)
    far = far_tile ^ far_source
    far_behind = far_source > far_tile

    def level_row(level, first, count):
        return weight_ref[base + level : base + level + 1, first : first + count]

    def own_half(scores, first, slot):
        chosen = jnp.broadcast_to(level_row(0, first, HALF), (ROWS, HALF))
        for bit in range(ROW_BITS):
            chosen = jnp.where(near >= 2**bit, level_row(1 + bit, first, HALF), chosen)
        chosen = jnp.where(behind, 0.0, chosen)
        spread = jnp.zeros((TILES, HALF), jnp.float32)
        for bit in range(BLOCK_BITS - 1 - ROW_BITS):
            spread = jnp.where(far >= 2**bit, level_row(1 + ROW_BITS + bit, first, HALF), spread)
        tile_ref[slot] = jnp.where(far_behind, 0.0, spread)
        rows = []
        for tile in range(TILES):
            weights = jnp.where(lane_tile == tile, chosen, tile_ref[slot, tile : tile + 1, :])
            rows.append(scores[tile * ROWS : (tile + 1) * ROWS] * weights)
        return jnp.concatenate(rows, axis=0).astype(jnp.bfloat16)

    def begin(block):
        rows = slice(block * BLOCK, (block + 1) * BLOCK)
        query = jnp.transpose(query_ref[rows, columns])
        return query, jnp.dot(key_ref[rows, columns], query, preferred_element_type=jnp.float32)

    def finish(block, begun):
        query, scores = begun
        start = block * BLOCK
        rows = slice(start, start + BLOCK)
        low = own_half(scores[:HALF, :HALF], start, 2 * block)
        high = own_half(scores[HALF:, HALF:], start + HALF, 2 * block + 1)
        across = (scores[:HALF, HALF:] * level_row(BLOCK_BITS, start + HALF, HALF)).astype(jnp.bfloat16)
        right = [
            jnp.concatenate([low, across], axis=1),
            jnp.concatenate([jnp.zeros_like(low), high], axis=1),
        ]
        left = [turned_ref[head, :, rows]]
        terms = [
            (BLOCK_BITS + 1 + bit, left_ref[head, (block >> bit << bit) - 1])
            for bit in range(block_count.bit_length() - 1)
            if block >> bit & 1
        ]
        for level, sibling in terms + states:
            scaled = query.astype(jnp.float32) * level_row(level, start, BLOCK)
            right.append(scaled.astype(jnp.bfloat16))
            left.append(sibling)
        part_ref[:, rows] = jnp.dot(
            jnp.concatenate(left, axis=1), jnp.concatenate(right, axis=0),
            preferred_element_type=jnp.float32,
        )

    pipelined(list(range(block_count)), begin, finish)


def remote_kernel(heads, levels, *refs):
    count = len(heads)
    weight_ref, query_ref = refs[:2]
    part_refs = refs[2 : 2 + count]
    state_refs = refs[2 + count : 2 + count + len(levels)]
    out_hbm, buffer, sems = refs[-3:]
    token_count = weight_ref.shape[1]
    size = token_count // PIECES
    states = [
        jnp.concatenate([ref[place] for ref in state_refs], axis=0).astype(jnp.bfloat16)
        for place in range(count)
    ]
    copies = []

    def begin(unit):
        start, place = unit
        columns = slice(heads[place] * LANES, (heads[place] + 1) * LANES)
        return lax.dot_general(
            states[place], query_ref[start : start + BLOCK, columns], ROW_BY_ROW,
            preferred_element_type=jnp.float32,
        )

    def finish(unit, product):
        start, place = unit
        rows = slice(start, start + BLOCK)
        result = part_refs[place][:, rows]
        for spot, level in enumerate(levels):
            row = heads[place] * SLOT + level
            result = result + product[spot * LANES : (spot + 1) * LANES] * weight_ref[row : row + 1, rows]
        buffer[rows, place * LANES : (place + 1) * LANES] = jnp.transpose(result.astype(buffer.dtype))
        if place + 1 == count and (start + BLOCK) % size == 0:
            piece = pl.ds(start + BLOCK - size, size)
            target = out_hbm.at[piece, pl.ds(heads[0] * LANES, count * LANES)]
            copies.append(pltpu.make_async_copy(buffer.at[piece, :], target, sems.at[len(copies)]))
            copies[-1].start()

    units = [(start, place) for start in range(0, token_count, BLOCK) for place in range(count)]
    pipelined(units, begin, finish)
    for copy in copies:
        copy.wait()


def join_kernel(left_ref, right_ref, *refs):
    refs[-1][...] = left_ref[...] + right_ref[...]


def join(total, received, after):
    return pl.pallas_call(
        join_kernel,
        in_specs=[VMEM, VMEM] + [ANY] * len(after),
        out_specs=VMEM,
        out_shape=jax.ShapeDtypeStruct(total.shape, total.dtype),
        compiler_params=pltpu.CompilerParams(vmem_limit_bytes=2 * MIB),
        name="join",
    )(total, received, *after)


def exchange(total, bit):
    devices = lax.axis_size("ctx")
    return lax.ppermute(total, "ctx", [(device, device ^ 2**bit) for device in range(devices)])


def body(queries, key_vectors, value_vectors, token_rows, weight_table):
    table_rows, head_count, level_count = weight_table.shape
    token_count = queries.shape[0]
    width = queries.shape[1] // head_count
    block_count = token_count // BLOCK
    local_bits = token_count.bit_length() - 1
    devices = lax.axis_size("ctx")
    bit_count = devices.bit_length() - 1
    group = head_count // GROUPS
    shape = jax.ShapeDtypeStruct
    whole = shape(queries.shape, queries.dtype)
    params = pltpu.CompilerParams(vmem_limit_bytes=8 * MIB)
    in_hbm = lambda array: pltpu.with_memory_space_constraint(array, pltpu.HBM)
    key_vectors, value_vectors = in_hbm(key_vectors), in_hbm(value_vectors)

    keys, turned, lefts, weights, *totals = pl.pallas_call(
        lambda *refs: totals_kernel(local_bits, *refs),
        in_specs=[HBM] * 4,
        out_specs=[VMEM] * (4 + GROUPS),
        out_shape=[
            whole,
            shape((head_count, width, token_count), jnp.bfloat16),
            shape((head_count, block_count, width, width), jnp.bfloat16),
            shape((head_count * SLOT, token_count), jnp.float32),
            *[shape((group, width, width), jnp.float32)] * GROUPS,
        ],
        scratch_shapes=[
            pltpu.VMEM(queries.shape, queries.dtype),
            pltpu.VMEM((1, token_count), jnp.int32),
            pltpu.VMEM((level_count, head_count, table_rows), jnp.float32),
            pltpu.SemaphoreType.DMA((PIECES, 2)),
            pltpu.SemaphoreType.DMA((2,)),
        ],
        compiler_params=params,
        name="totals",
    )(key_vectors, value_vectors, in_hbm(token_rows[None, :]), in_hbm(jnp.transpose(weight_table, (2, 1, 0))))

    def local(head, states):
        return pl.pallas_call(
            lambda *refs: local_kernel(head, head % group, local_bits, *refs),
            in_specs=[VMEM] * (5 + len(states)),
            out_specs=VMEM,
            out_shape=shape((width, token_count), jnp.float32),
            scratch_shapes=[pltpu.VMEM((2 * block_count, TILES, HALF), jnp.float32)],
            compiler_params=params,
            name="local",
        )(queries, keys, turned, lefts, weights, *states)

    received = [[exchange(total, 0)] for total in totals]
    parts, after = [], []
    for index, total in enumerate(totals):
        members = range(index * group, (index + 1) * group)
        if index == 0:
            parts += [local(head, []) for head in members]
        for bit in range(1, bit_count):
            total = join(total, received[index][-1], parts[index : index + 1])
            received[index].append(exchange(total, bit))
        if index:
            parts += [local(head, received[index][:-1]) for head in members]

    out = None
    for index, arrived in enumerate(received):
        heads = tuple(range(index * group, (index + 1) * group))
        first = bit_count - 1 if index else 0
        levels = tuple(range(local_bits + 1 + first, local_bits + 1 + bit_count))
        operands = [weights, queries] + [parts[head] for head in heads] + arrived[first:]
        out = pl.pallas_call(
            lambda *refs, heads=heads, levels=levels: remote_kernel(heads, levels, *refs),
            in_specs=[VMEM] * len(operands) + ([] if out is None else [HBM]),
            out_specs=HBM,
            out_shape=whole,
            input_output_aliases={} if out is None else {len(operands): 0},
            scratch_shapes=[
                pltpu.VMEM((token_count, group * width), jnp.bfloat16),
                pltpu.SemaphoreType.DMA((PIECES,)),
            ],
            compiler_params=params,
            name="remote",
        )(*operands, *(() if out is None else (out,)))
    return out


def solution(mesh):
    placed = (
        P(("groups", "ctx"), "head"),
        P(("groups", "ctx"), "head"),
        P(("groups", "ctx"), "head"),
        P(("groups", "ctx")),
        P(None, "head", None),
    )
    return jax.shard_map(
        body, mesh=mesh, in_specs=placed, out_specs=P(("groups", "ctx"), "head"), check_vma=False
    )
```

```python
import jax
import jax.numpy as jnp
from jax import lax
from jax.experimental import pallas as pl
from jax.experimental.pallas import tpu as pltpu
from jax.sharding import PartitionSpec as P

BLOCK = 256
HALF = BLOCK // 2
BLOCK_BITS = BLOCK.bit_length() - 1
ROWS = 8
ROW_BITS = ROWS.bit_length() - 1
TILES = HALF // ROWS
LANES = 128
SLOT = 32
PIECES = 8
GROUPS = 2
MIB = 1 << 20
VMEM = pl.BlockSpec(memory_space=pltpu.VMEM)
HBM = pl.BlockSpec(memory_space=pltpu.HBM)
ANY = pl.BlockSpec(memory_space=pl.ANY)
ROW_BY_ROW = (((1,), (1,)), ((), ()))


def level_weights(rows_ref, table_ref, weight_ref, local_bits):
    levels, heads, table_rows = table_ref.shape
    device = lax.axis_index("ctx")
    level = lax.broadcasted_iota(jnp.int32, (levels, table_rows), 0)
    scale = jnp.ones((levels, table_rows), jnp.float32)
    for level_id in range(2, levels):
        scale = jnp.where(level == level_id, 2.0 ** (-(level_id - 1) / 2), scale)
    for bit in range(lax.axis_size("ctx").bit_length() - 1):
        held = (device >> bit & 1).astype(jnp.float32)
        scale = jnp.where(level == local_bits + 1 + bit, scale * held, scale)
    slots = []
    for head in range(heads):
        slots.append(table_ref[:, head, :] * scale)
        slots.append(jnp.zeros((SLOT - levels, table_rows), jnp.float32))
    table = jnp.concatenate(slots, axis=0)
    high = table.astype(jnp.bfloat16)
    low = (table - high.astype(jnp.float32)).astype(jnp.bfloat16)
    ids = lax.broadcasted_iota(jnp.int32, (table_rows, BLOCK), 0)
    for start in range(0, weight_ref.shape[1], BLOCK):
        pick = (ids == rows_ref[:, start : start + BLOCK]).astype(jnp.float32).astype(jnp.bfloat16)
        weight_ref[:, start : start + BLOCK] = jnp.dot(
            high, pick, preferred_element_type=jnp.float32
        ) + jnp.dot(low, pick, preferred_element_type=jnp.float32)


def pipelined(units, begin, finish):
    ahead = begin(units[0])
    for unit, following in zip(units, units[1:] + [None]):
        held, ahead = ahead, None if following is None else begin(following)
        finish(unit, held)


def totals_kernel(key_hbm, value_hbm, key_ref, turned_ref, left_ref, *refs):
    total_refs = refs[:GROUPS]
    value_ref, sems = refs[GROUPS:]
    token_count = key_ref.shape[0]
    head_count = turned_ref.shape[0]
    group = head_count // GROUPS
    block_count = token_count // BLOCK
    size = token_count // PIECES
    blocks = block_count // PIECES
    copies = []
    for piece in range(PIECES):
        rows = pl.ds(piece * size, size)
        copies.append([
            pltpu.make_async_copy(source.at[rows, :], target.at[rows, :], sems.at[piece, which])
            for which, (source, target) in enumerate(((key_hbm, key_ref), (value_hbm, value_ref)))
        ])
    for pair in copies:
        for copy in pair:
            copy.start()

    held = [{} for _ in range(head_count)]

    def begin(unit):
        block, head = unit
        rows = slice(block * BLOCK, (block + 1) * BLOCK)
        turned = jnp.transpose(value_ref[rows, head * LANES : (head + 1) * LANES])
        turned_ref[head, :, rows] = turned
        return turned

    def finish(unit, turned):
        block, head = unit
        rows = slice(block * BLOCK, (block + 1) * BLOCK)
        carry = jnp.dot(
            turned, key_ref[rows, head * LANES : (head + 1) * LANES], preferred_element_type=jnp.float32
        )
        bit = 0
        while block >> bit & 1:
            carry = carry + held[head].pop(bit)
            bit += 1
        held[head][bit] = carry
        if block + 1 < block_count:
            left_ref[head, block] = carry.astype(jnp.bfloat16)
        else:
            total_refs[head // group][head % group] = carry

    for piece, pair in enumerate(copies):
        for copy in pair:
            copy.wait()
        span = range(piece * blocks, (piece + 1) * blocks)
        pipelined([(block, head) for block in span for head in range(head_count)], begin, finish)


def prepare_kernel(local_bits, after_ref, query_hbm, rows_hbm, table_hbm, weight_ref, query_ref, *refs):
    rows_ref, table_ref, sems = refs
    small = [
        pltpu.make_async_copy(rows_hbm, rows_ref, sems.at[0]),
        pltpu.make_async_copy(table_hbm, table_ref, sems.at[1]),
    ]
    large = pltpu.make_async_copy(query_hbm, query_ref, sems.at[2])
    for copy in small + [large]:
        copy.start()
    for copy in small:
        copy.wait()
    level_weights(rows_ref, table_ref, weight_ref, local_bits)
    large.wait()


def local_kernel(head, place, local_bits, *refs):
    query_ref, key_ref, turned_ref, left_ref, weight_ref = refs[:5]
    state_refs = refs[5:-2]
    part_ref, tile_ref = refs[-2:]
    token_count = query_ref.shape[0]
    block_count = token_count // BLOCK
    columns = slice(head * LANES, (head + 1) * LANES)
    base = head * SLOT
    states = [(local_bits + 1 + bit, ref[place].astype(jnp.bfloat16)) for bit, ref in enumerate(state_refs)]

    lane = lax.broadcasted_iota(jnp.int32, (ROWS, HALF), 1)
    source = lax.broadcasted_iota(jnp.int32, (ROWS, HALF), 0)
    lane_tile = lane >> ROW_BITS
    near = (lane & ROWS - 1) ^ source
    behind = source > (lane & ROWS - 1)
    far_tile = lax.broadcasted_iota(jnp.int32, (TILES, HALF), 1) >> ROW_BITS
    far_source = lax.broadcasted_iota(jnp.int32, (TILES, HALF), 0)
    far = far_tile ^ far_source
    far_behind = far_source > far_tile

    def level_row(level, first, count):
        return weight_ref[base + level : base + level + 1, first : first + count]

    def own_half(scores, first, slot):
        chosen = jnp.broadcast_to(level_row(0, first, HALF), (ROWS, HALF))
        for bit in range(ROW_BITS):
            chosen = jnp.where(near >= 2**bit, level_row(1 + bit, first, HALF), chosen)
        chosen = jnp.where(behind, 0.0, chosen)
        spread = jnp.zeros((TILES, HALF), jnp.float32)
        for bit in range(BLOCK_BITS - 1 - ROW_BITS):
            spread = jnp.where(far >= 2**bit, level_row(1 + ROW_BITS + bit, first, HALF), spread)
        tile_ref[slot] = jnp.where(far_behind, 0.0, spread)
        rows = []
        for tile in range(TILES):
            weights = jnp.where(lane_tile == tile, chosen, tile_ref[slot, tile : tile + 1, :])
            rows.append(scores[tile * ROWS : (tile + 1) * ROWS] * weights)
        return jnp.concatenate(rows, axis=0).astype(jnp.bfloat16)

    def begin(block):
        rows = slice(block * BLOCK, (block + 1) * BLOCK)
        query = jnp.transpose(query_ref[rows, columns])
        return query, jnp.dot(key_ref[rows, columns], query, preferred_element_type=jnp.float32)

    def finish(block, begun):
        query, scores = begun
        start = block * BLOCK
        rows = slice(start, start + BLOCK)
        low = own_half(scores[:HALF, :HALF], start, 2 * block)
        high = own_half(scores[HALF:, HALF:], start + HALF, 2 * block + 1)
        across = (scores[:HALF, HALF:] * level_row(BLOCK_BITS, start + HALF, HALF)).astype(jnp.bfloat16)
        right = [
            jnp.concatenate([low, across], axis=1),
            jnp.concatenate([jnp.zeros_like(low), high], axis=1),
        ]
        left = [turned_ref[head, :, rows]]
        terms = [
            (BLOCK_BITS + 1 + bit, left_ref[head, (block >> bit << bit) - 1])
            for bit in range(block_count.bit_length() - 1)
            if block >> bit & 1
        ]
        for level, sibling in terms + states:
            scaled = query.astype(jnp.float32) * level_row(level, start, BLOCK)
            right.append(scaled.astype(jnp.bfloat16))
            left.append(sibling)
        part_ref[:, rows] = jnp.dot(
            jnp.concatenate(left, axis=1), jnp.concatenate(right, axis=0),
            preferred_element_type=jnp.float32,
        )

    pipelined(list(range(block_count)), begin, finish)


def remote_kernel(heads, level, *refs):
    count = len(heads)
    weight_ref, query_ref = refs[:2]
    part_refs = refs[2 : 2 + count]
    state_ref = refs[2 + count]
    out_hbm, buffer, sems = refs[-3:]
    token_count = weight_ref.shape[1]
    size = token_count // PIECES
    states = [state_ref[place].astype(jnp.bfloat16) for place in range(count)]
    copies = []

    def begin(unit):
        start, place = unit
        columns = slice(heads[place] * LANES, (heads[place] + 1) * LANES)
        return lax.dot_general(
            states[place], query_ref[start : start + BLOCK, columns], ROW_BY_ROW,
            preferred_element_type=jnp.float32,
        )

    def finish(unit, product):
        start, place = unit
        rows = slice(start, start + BLOCK)
        row = heads[place] * SLOT + level
        result = part_refs[place][:, rows] + product * weight_ref[row : row + 1, rows]
        buffer[rows, place * LANES : (place + 1) * LANES] = jnp.transpose(result.astype(buffer.dtype))
        if place + 1 == count and (start + BLOCK) % size == 0:
            piece = pl.ds(start + BLOCK - size, size)
            target = out_hbm.at[piece, pl.ds(heads[0] * LANES, count * LANES)]
            copies.append(pltpu.make_async_copy(buffer.at[piece, :], target, sems.at[len(copies)]))
            copies[-1].start()

    units = [(start, place) for start in range(0, token_count, BLOCK) for place in range(count)]
    pipelined(units, begin, finish)
    for copy in copies:
        copy.wait()


def join_kernel(left_ref, right_ref, after_ref, out_ref):
    out_ref[...] = left_ref[...] + right_ref[...]


def join(total, received, after):
    return pl.pallas_call(
        join_kernel,
        in_specs=[VMEM, VMEM, ANY],
        out_specs=VMEM,
        out_shape=jax.ShapeDtypeStruct(total.shape, total.dtype),
        compiler_params=pltpu.CompilerParams(vmem_limit_bytes=2 * MIB),
        name="join",
    )(total, received, after)


def gate_kernel(total_ref, after_ref, out_ref):
    out_ref[...] = total_ref[...]


def gate(total, after):
    return pl.pallas_call(
        gate_kernel,
        in_specs=[VMEM, ANY],
        out_specs=VMEM,
        out_shape=jax.ShapeDtypeStruct(total.shape, total.dtype),
        compiler_params=pltpu.CompilerParams(vmem_limit_bytes=2 * MIB),
        name="gate",
    )(total, after)


def exchange(total, bit):
    devices = lax.axis_size("ctx")
    return lax.ppermute(total, "ctx", [(device, device ^ 2**bit) for device in range(devices)])


def body(queries, key_vectors, value_vectors, token_rows, weight_table):
    table_rows, head_count, level_count = weight_table.shape
    token_count = queries.shape[0]
    width = queries.shape[1] // head_count
    block_count = token_count // BLOCK
    local_bits = token_count.bit_length() - 1
    devices = lax.axis_size("ctx")
    bit_count = devices.bit_length() - 1
    group = head_count // GROUPS
    shape = jax.ShapeDtypeStruct
    whole = shape(queries.shape, queries.dtype)
    params = pltpu.CompilerParams(vmem_limit_bytes=8 * MIB)
    in_hbm = lambda array: pltpu.with_memory_space_constraint(array, pltpu.HBM)
    queries, key_vectors, value_vectors = in_hbm(queries), in_hbm(key_vectors), in_hbm(value_vectors)

    keys, turned, lefts, *totals = pl.pallas_call(
        totals_kernel,
        in_specs=[HBM] * 2,
        out_specs=[VMEM] * (3 + GROUPS),
        out_shape=[
            whole,
            shape((head_count, width, token_count), jnp.bfloat16),
            shape((head_count, block_count, width, width), jnp.bfloat16),
            *[shape((group, width, width), jnp.float32)] * GROUPS,
        ],
        scratch_shapes=[
            pltpu.VMEM(queries.shape, queries.dtype),
            pltpu.SemaphoreType.DMA((PIECES, 2)),
        ],
        compiler_params=params,
        name="totals",
    )(key_vectors, value_vectors)

    weights, query = pl.pallas_call(
        lambda *refs: prepare_kernel(local_bits, *refs),
        in_specs=[ANY] + [HBM] * 3,
        out_specs=[VMEM] * 2,
        out_shape=[shape((head_count * SLOT, token_count), jnp.float32), whole],
        scratch_shapes=[
            pltpu.VMEM((1, token_count), jnp.int32),
            pltpu.VMEM((level_count, head_count, table_rows), jnp.float32),
            pltpu.SemaphoreType.DMA((3,)),
        ],
        compiler_params=params,
        name="prepare",
    )(lefts, queries, in_hbm(token_rows[None, :]), in_hbm(jnp.transpose(weight_table, (2, 1, 0))))

    totals[1:] = [gate(total, weights) for total in totals[1:]]
    received = [[exchange(total, 0)] for total in totals]
    parts = []
    after = weights
    for index, total in enumerate(totals):
        for bit in range(1, bit_count):
            total = join(total, received[index][-1], after)
            received[index].append(exchange(total, bit))
        for head in range(index * group, (index + 1) * group):
            parts += pl.pallas_call(
                lambda *refs, head=head: local_kernel(head, head % group, local_bits, *refs),
                in_specs=[VMEM] * (5 + bit_count - 1),
                out_specs=[VMEM],
                out_shape=[shape((width, token_count), jnp.float32)],
                scratch_shapes=[pltpu.VMEM((2 * block_count, TILES, HALF), jnp.float32)],
                compiler_params=params,
                name="local",
            )(query, keys, turned, lefts, weights, *received[index][:-1])
        after = parts[0]

    out = None
    for index, arrived in enumerate(received):
        heads = tuple(range(index * group, (index + 1) * group))
        operands = [weights, query] + [parts[head] for head in heads] + [arrived[-1]]
        out = pl.pallas_call(
            lambda *refs, heads=heads: remote_kernel(heads, local_bits + bit_count, *refs),
            in_specs=[VMEM] * len(operands) + ([] if out is None else [HBM]),
            out_specs=HBM,
            out_shape=whole,
            input_output_aliases={} if out is None else {len(operands): 0},
            scratch_shapes=[
                pltpu.VMEM((token_count, group * width), jnp.bfloat16),
                pltpu.SemaphoreType.DMA((PIECES,)),
            ],
            compiler_params=params,
            name="remote",
        )(*operands, *(() if out is None else (out,)))
    return out


def solution(mesh):
    placed = (
        P(("groups", "ctx"), "head"),
        P(("groups", "ctx"), "head"),
        P(("groups", "ctx"), "head"),
        P(("groups", "ctx")),
        P(None, "head", None),
    )
    return jax.shard_map(
        body, mesh=mesh, in_specs=placed, out_specs=P(("groups", "ctx"), "head"), check_vma=False
    )
```

```python
import jax
import jax.numpy as jnp
from jax import lax
from jax.experimental import pallas as pl
from jax.experimental.pallas import tpu as pltpu
from jax.sharding import PartitionSpec as P


BLOCK = 256
HALF = BLOCK // 2
BLOCK_BITS = BLOCK.bit_length() - 1
ROWS = 8
ROW_BITS = ROWS.bit_length() - 1
TILES = HALF // ROWS
LANES = 128
SLOT = 32
PIECES = 8
DEPTH = 3
MIB = 1 << 20
VMEM = pl.BlockSpec(memory_space=pltpu.VMEM)
HBM = pl.BlockSpec(memory_space=pltpu.HBM)
ANY = pl.BlockSpec(memory_space=pl.ANY)
ROW_BY_ROW = (((1,), (1,)), ((), ()))


def level_weights(rows_ref, table_ref, weight_ref, local_bits):
    levels, heads, table_rows = table_ref.shape
    device = lax.axis_index("ctx")
    level = lax.broadcasted_iota(jnp.int32, (levels, table_rows), 0)
    scale = jnp.ones((levels, table_rows), jnp.float32)
    for level_id in range(2, levels):
        scale = jnp.where(level == level_id, 2.0 ** (-(level_id - 1) / 2), scale)
    for bit in range(lax.axis_size("ctx").bit_length() - 1):
        held = (device >> bit & 1).astype(jnp.float32)
        scale = jnp.where(level == local_bits + 1 + bit, scale * held, scale)
    slots = []
    for head in range(heads):
        slots.append(table_ref[:, head, :] * scale)
        slots.append(jnp.zeros((SLOT - levels, table_rows), jnp.float32))
    table = jnp.concatenate(slots, axis=0)
    high = table.astype(jnp.bfloat16)
    low = (table - high.astype(jnp.float32)).astype(jnp.bfloat16)
    ids = lax.broadcasted_iota(jnp.int32, (table_rows, BLOCK), 0)
    for start in range(0, weight_ref.shape[1], BLOCK):
        pick = (ids == rows_ref[:, start : start + BLOCK]).astype(jnp.float32).astype(jnp.bfloat16)
        weight_ref[:, start : start + BLOCK] = jnp.dot(
            high, pick, preferred_element_type=jnp.float32
        ) + jnp.dot(low, pick, preferred_element_type=jnp.float32)


def pipelined(units, begin, finish, depth=1):
    begun = [begin(unit) for unit in units[:depth]]
    for index, unit in enumerate(units):
        if index + depth < len(units):
            begun.append(begin(units[index + depth]))
        finish(unit, begun[index])


def totals_kernel(home, key_hbm, value_hbm, key_ref, turned_ref, left_ref, *refs):
    total_refs = refs[:-2]
    value_ref, sems = refs[-2:]
    token_count = key_ref.shape[0]
    head_count = turned_ref.shape[0]
    block_count = token_count // BLOCK
    size = token_count // PIECES
    blocks = block_count // PIECES
    copies = []
    for piece in range(PIECES):
        rows = pl.ds(piece * size, size)
        copies.append([
            pltpu.make_async_copy(source.at[rows, :], target.at[rows, :], sems.at[piece, which])
            for which, (source, target) in enumerate(((key_hbm, key_ref), (value_hbm, value_ref)))
        ])
    for pair in copies:
        for copy in pair:
            copy.start()

    held = [{} for _ in range(head_count)]

    def begin(unit):
        block, head = unit
        rows = slice(block * BLOCK, (block + 1) * BLOCK)
        turned = jnp.transpose(value_ref[rows, head * LANES : (head + 1) * LANES])
        turned_ref[head, :, rows] = turned
        return turned

    def finish(unit, turned):
        block, head = unit
        rows = slice(block * BLOCK, (block + 1) * BLOCK)
        carry = jnp.dot(
            turned, key_ref[rows, head * LANES : (head + 1) * LANES], preferred_element_type=jnp.float32
        )
        bit = 0
        while block >> bit & 1:
            carry = carry + held[head].pop(bit)
            bit += 1
        held[head][bit] = carry
        if block + 1 < block_count:
            left_ref[head, block] = carry.astype(jnp.bfloat16)
        else:
            total_refs[home[head][0]][home[head][1]] = carry

    for piece, pair in enumerate(copies):
        for copy in pair:
            copy.wait()
        span = range(piece * blocks, (piece + 1) * blocks)
        pipelined([(block, head) for block in span for head in range(head_count)], begin, finish)


def prepare_kernel(local_bits, after_ref, query_hbm, rows_hbm, table_hbm, weight_ref, query_ref, *refs):
    rows_ref, table_ref, sems = refs
    small = [
        pltpu.make_async_copy(rows_hbm, rows_ref, sems.at[0]),
        pltpu.make_async_copy(table_hbm, table_ref, sems.at[1]),
    ]
    large = pltpu.make_async_copy(query_hbm, query_ref, sems.at[2])
    for copy in small + [large]:
        copy.start()
    for copy in small:
        copy.wait()
    level_weights(rows_ref, table_ref, weight_ref, local_bits)
    large.wait()


def local_kernel(head, place, local_bits, *refs):
    query_ref, key_ref, turned_ref, left_ref, weight_ref = refs[:5]
    state_refs = refs[5:-2]
    part_ref, tile_ref = refs[-2:]
    token_count = query_ref.shape[0]
    block_count = token_count // BLOCK
    columns = slice(head * LANES, (head + 1) * LANES)
    base = head * SLOT
    states = [(local_bits + 1 + bit, ref[place].astype(jnp.bfloat16)) for bit, ref in enumerate(state_refs)]

    lane = lax.broadcasted_iota(jnp.int32, (ROWS, HALF), 1)
    source = lax.broadcasted_iota(jnp.int32, (ROWS, HALF), 0)
    lane_tile = lane >> ROW_BITS
    near = (lane & ROWS - 1) ^ source
    behind = source > (lane & ROWS - 1)
    far_tile = lax.broadcasted_iota(jnp.int32, (TILES, HALF), 1) >> ROW_BITS
    far_source = lax.broadcasted_iota(jnp.int32, (TILES, HALF), 0)
    far = far_tile ^ far_source
    far_behind = far_source > far_tile

    def level_row(level, first, count):
        return weight_ref[base + level : base + level + 1, first : first + count]

    def own_half(scores, first, slot):
        chosen = jnp.broadcast_to(level_row(0, first, HALF), (ROWS, HALF))
        for bit in range(ROW_BITS):
            chosen = jnp.where(near >= 2**bit, level_row(1 + bit, first, HALF), chosen)
        chosen = jnp.where(behind, 0.0, chosen)
        spread = jnp.zeros((TILES, HALF), jnp.float32)
        for bit in range(BLOCK_BITS - 1 - ROW_BITS):
            spread = jnp.where(far >= 2**bit, level_row(1 + ROW_BITS + bit, first, HALF), spread)
        tile_ref[slot] = jnp.where(far_behind, 0.0, spread)
        rows = []
        for tile in range(TILES):
            weights = jnp.where(lane_tile == tile, chosen, tile_ref[slot, tile : tile + 1, :])
            rows.append(scores[tile * ROWS : (tile + 1) * ROWS] * weights)
        return jnp.concatenate(rows, axis=0).astype(jnp.bfloat16)

    def begin(block):
        rows = slice(block * BLOCK, (block + 1) * BLOCK)
        query = jnp.transpose(query_ref[rows, columns])
        return query, jnp.dot(key_ref[rows, columns], query, preferred_element_type=jnp.float32)

    def finish(block, begun):
        query, scores = begun
        start = block * BLOCK
        rows = slice(start, start + BLOCK)
        low = own_half(scores[:HALF, :HALF], start, 2 * block)
        high = own_half(scores[HALF:, HALF:], start + HALF, 2 * block + 1)
        across = (scores[:HALF, HALF:] * level_row(BLOCK_BITS, start + HALF, HALF)).astype(jnp.bfloat16)
        right = [
            jnp.concatenate([low, across], axis=1),
            jnp.concatenate([jnp.zeros_like(low), high], axis=1),
        ]
        left = [turned_ref[head, :, rows]]
        terms = [
            (BLOCK_BITS + 1 + bit, left_ref[head, (block >> bit << bit) - 1])
            for bit in range(block_count.bit_length() - 1)
            if block >> bit & 1
        ]
        for level, sibling in terms + states:
            scaled = query.astype(jnp.float32) * level_row(level, start, BLOCK)
            right.append(scaled.astype(jnp.bfloat16))
            left.append(sibling)
        part_ref[:, rows] = jnp.dot(
            jnp.concatenate(left, axis=1), jnp.concatenate(right, axis=0),
            preferred_element_type=jnp.float32,
        )

    pipelined(list(range(block_count)), begin, finish, DEPTH)


def remote_kernel(heads, places, level, *refs):
    count = len(heads)
    weight_ref, query_ref = refs[:2]
    part_refs = refs[2 : 2 + count]
    state_refs = refs[2 + count : 2 + 2 * count]
    out_hbm, buffer, sems = refs[-3:]
    token_count = weight_ref.shape[1]
    size = token_count // PIECES
    states = [ref[place].astype(jnp.bfloat16) for ref, place in zip(state_refs, places)]
    copies = []

    def begin(unit):
        start, place = unit
        columns = slice(heads[place] * LANES, (heads[place] + 1) * LANES)
        return lax.dot_general(
            states[place], query_ref[start : start + BLOCK, columns], ROW_BY_ROW,
            preferred_element_type=jnp.float32,
        )

    def finish(unit, product):
        start, place = unit
        rows = slice(start, start + BLOCK)
        row = heads[place] * SLOT + level
        result = part_refs[place][:, rows] + product * weight_ref[row : row + 1, rows]
        buffer[rows, place * LANES : (place + 1) * LANES] = jnp.transpose(result.astype(buffer.dtype))
        if place + 1 == count and (start + BLOCK) % size == 0:
            piece = pl.ds(start + BLOCK - size, size)
            target = out_hbm.at[piece, pl.ds(heads[0] * LANES, count * LANES)]
            copies.append(pltpu.make_async_copy(buffer.at[piece, :], target, sems.at[len(copies)]))
            copies[-1].start()

    units = [(start, place) for start in range(0, token_count, BLOCK) for place in range(count)]
    pipelined(units, begin, finish)
    for copy in copies:
        copy.wait()


def join_kernel(left_ref, right_ref, after_ref, out_ref):
    out_ref[...] = left_ref[...] + right_ref[...]


def join(total, received, after):
    return pl.pallas_call(
        join_kernel,
        in_specs=[VMEM, VMEM, ANY],
        out_specs=VMEM,
        out_shape=jax.ShapeDtypeStruct(total.shape, total.dtype),
        compiler_params=pltpu.CompilerParams(vmem_limit_bytes=2 * MIB),
        name="join",
    )(total, received, after)


def exchange(total, bit):
    devices = lax.axis_size("ctx")
    pairs = [(device, device ^ 2**bit) for device in range(devices)]
    return lax.ppermute(total, "ctx", pairs)


def groups_of(head_count):
    half = head_count // 2
    firsts = sorted({0, half // 2, half})
    return [range(first, last) for first, last in zip(firsts, firsts[1:] + [head_count])]


def body(queries, key_vectors, value_vectors, token_rows, weight_table):
    table_rows, head_count, level_count = weight_table.shape
    token_count = queries.shape[0]
    width = queries.shape[1] // head_count
    block_count = token_count // BLOCK
    local_bits = token_count.bit_length() - 1
    devices = lax.axis_size("ctx")
    bit_count = devices.bit_length() - 1
    half = head_count // 2
    groups = groups_of(head_count)
    home = {head: (index, head - heads[0]) for index, heads in enumerate(groups) for head in heads}
    shape = jax.ShapeDtypeStruct
    whole = shape(queries.shape, queries.dtype)
    params = pltpu.CompilerParams(vmem_limit_bytes=8 * MIB)
    in_hbm = lambda array: pltpu.with_memory_space_constraint(array, pltpu.HBM)
    queries, key_vectors, value_vectors = in_hbm(queries), in_hbm(key_vectors), in_hbm(value_vectors)

    keys, turned, lefts, *totals = pl.pallas_call(
        lambda *refs: totals_kernel(home, *refs),
        in_specs=[HBM] * 2,
        out_specs=[VMEM] * (3 + len(groups)),
        out_shape=[
            whole,
            shape((head_count, width, token_count), jnp.bfloat16),
            shape((head_count, block_count, width, width), jnp.bfloat16),
            *[shape((len(heads), width, width), jnp.float32) for heads in groups],
        ],
        scratch_shapes=[
            pltpu.VMEM(queries.shape, queries.dtype),
            pltpu.SemaphoreType.DMA((PIECES, 2)),
        ],
        compiler_params=params,
        name="totals",
    )(key_vectors, value_vectors)

    weights, query = pl.pallas_call(
        lambda *refs: prepare_kernel(local_bits, *refs),
        in_specs=[ANY] + [HBM] * 3,
        out_specs=[VMEM] * 2,
        out_shape=[shape((head_count * SLOT, token_count), jnp.float32), whole],
        scratch_shapes=[
            pltpu.VMEM((1, token_count), jnp.int32),
            pltpu.VMEM((level_count, head_count, table_rows), jnp.float32),
            pltpu.SemaphoreType.DMA((3,)),
        ],
        compiler_params=params,
        name="prepare",
    )(lefts, queries, in_hbm(token_rows[None, :]), in_hbm(jnp.transpose(weight_table, (2, 1, 0))))

    received = [[exchange(total, 0)] for total in totals]
    parts = []
    after = weights
    for index, total in enumerate(totals):
        if index == len(groups) - 1:
            after = parts[0]
        for bit in range(1, bit_count):
            total = join(total, received[index][-1], after)
            received[index].append(exchange(total, bit))
        for head in groups[index]:
            local = pl.pallas_call(
                lambda *refs, head=head: local_kernel(head, home[head][1], local_bits, *refs),
                in_specs=[VMEM] * (5 + bit_count - 1),
                out_specs=[VMEM],
                out_shape=[shape((width, token_count), jnp.float32)],
                scratch_shapes=[pltpu.VMEM((2 * block_count, TILES, HALF), jnp.float32)],
                compiler_params=params,
                name="local",
            )
            parts += local(query, keys, turned, lefts, weights, *received[index][:-1])

    out = None
    for first in range(0, head_count, half):
        heads = tuple(range(first, first + half))
        places = tuple(home[head][1] for head in heads)
        operands = [weights, query] + [parts[head] for head in heads]
        operands += [received[home[head][0]][-1] for head in heads]
        out = pl.pallas_call(
            lambda *refs, heads=heads, places=places: remote_kernel(heads, places, local_bits + bit_count, *refs),
            in_specs=[VMEM] * len(operands) + ([] if out is None else [HBM]),
            out_specs=HBM,
            out_shape=whole,
            input_output_aliases={} if out is None else {len(operands): 0},
            scratch_shapes=[
                pltpu.VMEM((token_count, half * width), jnp.bfloat16),
                pltpu.SemaphoreType.DMA((PIECES,)),
            ],
            compiler_params=params,
            name="remote",
        )(*operands, *(() if out is None else (out,)))
    return out


def solution(mesh):
    placed = (
        P(("groups", "ctx"), "head"),
        P(("groups", "ctx"), "head"),
        P(("groups", "ctx"), "head"),
        P(("groups", "ctx")),
        P(None, "head", None),
    )

    return jax.shard_map(body, mesh=mesh, in_specs=placed, out_specs=P(("groups", "ctx"), "head"), check_vma=False)
```

```python
import jax
import jax.numpy as jnp
from jax import lax
from jax.experimental import pallas as pl
from jax.experimental.pallas import tpu as pltpu
from jax.sharding import PartitionSpec as P

BLOCK = 256
HALF = BLOCK // 2
BLOCK_BITS = BLOCK.bit_length() - 1
ROWS = 8
ROW_BITS = ROWS.bit_length() - 1
TILES = HALF // ROWS
LANES = 128
SLOT = 32
PIECES = 8
GROUPS = 2
DEPTH = 3
MIB = 1 << 20
VMEM = pl.BlockSpec(memory_space=pltpu.VMEM)
HBM = pl.BlockSpec(memory_space=pltpu.HBM)
ANY = pl.BlockSpec(memory_space=pl.ANY)
ROW_BY_ROW = (((1,), (1,)), ((), ()))


def level_weights(rows_ref, table_ref, weight_ref, local_bits):
    levels, heads, table_rows = table_ref.shape
    device = lax.axis_index("ctx")
    level = lax.broadcasted_iota(jnp.int32, (levels, table_rows), 0)
    scale = jnp.ones((levels, table_rows), jnp.float32)
    for level_id in range(2, levels):
        scale = jnp.where(level == level_id, 2.0 ** (-(level_id - 1) / 2), scale)
    for bit in range(lax.axis_size("ctx").bit_length() - 1):
        held = (device >> bit & 1).astype(jnp.float32)
        scale = jnp.where(level == local_bits + 1 + bit, scale * held, scale)
    slots = []
    for head in range(heads):
        slots.append(table_ref[:, head, :] * scale)
        slots.append(jnp.zeros((SLOT - levels, table_rows), jnp.float32))
    table = jnp.concatenate(slots, axis=0)
    high = table.astype(jnp.bfloat16)
    low = (table - high.astype(jnp.float32)).astype(jnp.bfloat16)
    ids = lax.broadcasted_iota(jnp.int32, (table_rows, BLOCK), 0)
    for start in range(0, weight_ref.shape[1], BLOCK):
        pick = (ids == rows_ref[:, start : start + BLOCK]).astype(jnp.float32).astype(jnp.bfloat16)
        weight_ref[:, start : start + BLOCK] = jnp.dot(
            high, pick, preferred_element_type=jnp.float32
        ) + jnp.dot(low, pick, preferred_element_type=jnp.float32)


def pipelined(units, begin, finish, depth=1):
    begun = [begin(unit) for unit in units[:depth]]
    for index, unit in enumerate(units):
        if index + depth < len(units):
            begun.append(begin(units[index + depth]))
        finish(unit, begun[index])


def totals_kernel(key_hbm, value_hbm, key_ref, turned_ref, left_ref, *refs):
    total_refs = refs[:GROUPS]
    value_ref, sems = refs[GROUPS:]
    token_count = key_ref.shape[0]
    head_count = turned_ref.shape[0]
    group = head_count // GROUPS
    block_count = token_count // BLOCK
    size = token_count // PIECES
    blocks = block_count // PIECES
    copies = []
    for piece in range(PIECES):
        rows = pl.ds(piece * size, size)
        copies.append([
            pltpu.make_async_copy(source.at[rows, :], target.at[rows, :], sems.at[piece, which])
            for which, (source, target) in enumerate(((key_hbm, key_ref), (value_hbm, value_ref)))
        ])
    for pair in copies:
        for copy in pair:
            copy.start()

    held = [{} for _ in range(head_count)]

    def begin(unit):
        block, head = unit
        rows = slice(block * BLOCK, (block + 1) * BLOCK)
        turned = jnp.transpose(value_ref[rows, head * LANES : (head + 1) * LANES])
        turned_ref[head, :, rows] = turned
        return turned

    def finish(unit, turned):
        block, head = unit
        rows = slice(block * BLOCK, (block + 1) * BLOCK)
        carry = jnp.dot(
            turned, key_ref[rows, head * LANES : (head + 1) * LANES], preferred_element_type=jnp.float32
        )
        bit = 0
        while block >> bit & 1:
            carry = carry + held[head].pop(bit)
            bit += 1
        held[head][bit] = carry
        if block + 1 < block_count:
            left_ref[head, block] = carry.astype(jnp.bfloat16)
        else:
            total_refs[head // group][head % group] = carry

    for piece, pair in enumerate(copies):
        for copy in pair:
            copy.wait()
        span = range(piece * blocks, (piece + 1) * blocks)
        pipelined([(block, head) for block in span for head in range(head_count)], begin, finish)


def prepare_kernel(local_bits, after_ref, query_hbm, rows_hbm, table_hbm, weight_ref, query_ref, *refs):
    rows_ref, table_ref, sems = refs
    small = [
        pltpu.make_async_copy(rows_hbm, rows_ref, sems.at[0]),
        pltpu.make_async_copy(table_hbm, table_ref, sems.at[1]),
    ]
    large = pltpu.make_async_copy(query_hbm, query_ref, sems.at[2])
    for copy in small + [large]:
        copy.start()
    for copy in small:
        copy.wait()
    level_weights(rows_ref, table_ref, weight_ref, local_bits)
    large.wait()


def local_kernel(head, place, local_bits, *refs):
    query_ref, key_ref, turned_ref, left_ref, weight_ref = refs[:5]
    state_refs = refs[5:-2]
    part_ref, tile_ref = refs[-2:]
    token_count = query_ref.shape[0]
    block_count = token_count // BLOCK
    columns = slice(head * LANES, (head + 1) * LANES)
    base = head * SLOT
    states = [(local_bits + 1 + bit, ref[place].astype(jnp.bfloat16)) for bit, ref in enumerate(state_refs)]

    lane = lax.broadcasted_iota(jnp.int32, (ROWS, HALF), 1)
    source = lax.broadcasted_iota(jnp.int32, (ROWS, HALF), 0)
    lane_tile = lane >> ROW_BITS
    near = (lane & ROWS - 1) ^ source
    behind = source > (lane & ROWS - 1)
    far_tile = lax.broadcasted_iota(jnp.int32, (TILES, HALF), 1) >> ROW_BITS
    far_source = lax.broadcasted_iota(jnp.int32, (TILES, HALF), 0)
    far = far_tile ^ far_source
    far_behind = far_source > far_tile

    def level_row(level, first, count):
        return weight_ref[base + level : base + level + 1, first : first + count]

    def own_half(scores, first, slot):
        chosen = jnp.broadcast_to(level_row(0, first, HALF), (ROWS, HALF))
        for bit in range(ROW_BITS):
            chosen = jnp.where(near >= 2**bit, level_row(1 + bit, first, HALF), chosen)
        chosen = jnp.where(behind, 0.0, chosen)
        spread = jnp.zeros((TILES, HALF), jnp.float32)
        for bit in range(BLOCK_BITS - 1 - ROW_BITS):
            spread = jnp.where(far >= 2**bit, level_row(1 + ROW_BITS + bit, first, HALF), spread)
        tile_ref[slot] = jnp.where(far_behind, 0.0, spread)
        rows = []
        for tile in range(TILES):
            weights = jnp.where(lane_tile == tile, chosen, tile_ref[slot, tile : tile + 1, :])
            rows.append(scores[tile * ROWS : (tile + 1) * ROWS] * weights)
        return jnp.concatenate(rows, axis=0).astype(jnp.bfloat16)

    def begin(block):
        rows = slice(block * BLOCK, (block + 1) * BLOCK)
        query = jnp.transpose(query_ref[rows, columns])
        return query, jnp.dot(key_ref[rows, columns], query, preferred_element_type=jnp.float32)

    def finish(block, begun):
        query, scores = begun
        start = block * BLOCK
        rows = slice(start, start + BLOCK)
        low = own_half(scores[:HALF, :HALF], start, 2 * block)
        high = own_half(scores[HALF:, HALF:], start + HALF, 2 * block + 1)
        across = (scores[:HALF, HALF:] * level_row(BLOCK_BITS, start + HALF, HALF)).astype(jnp.bfloat16)
        right = [
            jnp.concatenate([low, across], axis=1),
            jnp.concatenate([jnp.zeros_like(low), high], axis=1),
        ]
        left = [turned_ref[head, :, rows]]
        terms = [
            (BLOCK_BITS + 1 + bit, left_ref[head, (block >> bit << bit) - 1])
            for bit in range(block_count.bit_length() - 1)
            if block >> bit & 1
        ]
        for level, sibling in terms + states:
            scaled = query.astype(jnp.float32) * level_row(level, start, BLOCK)
            right.append(scaled.astype(jnp.bfloat16))
            left.append(sibling)
        part_ref[:, rows] = jnp.dot(
            jnp.concatenate(left, axis=1), jnp.concatenate(right, axis=0),
            preferred_element_type=jnp.float32,
        )

    pipelined(list(range(block_count)), begin, finish, DEPTH)


def remote_kernel(heads, level, *refs):
    count = len(heads)
    weight_ref, query_ref = refs[:2]
    part_refs = refs[2 : 2 + count]
    state_ref = refs[2 + count]
    out_hbm, buffer, sems = refs[-3:]
    token_count = weight_ref.shape[1]
    size = token_count // PIECES
    states = [state_ref[place].astype(jnp.bfloat16) for place in range(count)]
    copies = []

    def begin(unit):
        start, place = unit
        columns = slice(heads[place] * LANES, (heads[place] + 1) * LANES)
        return lax.dot_general(
            states[place], query_ref[start : start + BLOCK, columns], ROW_BY_ROW,
            preferred_element_type=jnp.float32,
        )

    def finish(unit, product):
        start, place = unit
        rows = slice(start, start + BLOCK)
        row = heads[place] * SLOT + level
        result = part_refs[place][:, rows] + product * weight_ref[row : row + 1, rows]
        buffer[rows, place * LANES : (place + 1) * LANES] = jnp.transpose(result.astype(buffer.dtype))
        if place + 1 == count and (start + BLOCK) % size == 0:
            piece = pl.ds(start + BLOCK - size, size)
            target = out_hbm.at[piece, pl.ds(heads[0] * LANES, count * LANES)]
            copies.append(pltpu.make_async_copy(buffer.at[piece, :], target, sems.at[len(copies)]))
            copies[-1].start()

    units = [(start, place) for start in range(0, token_count, BLOCK) for place in range(count)]
    pipelined(units, begin, finish)
    for copy in copies:
        copy.wait()


def join_kernel(left_ref, right_ref, after_ref, out_ref):
    out_ref[...] = left_ref[...] + right_ref[...]


def join(total, received, after):
    return pl.pallas_call(
        join_kernel,
        in_specs=[VMEM, VMEM, ANY],
        out_specs=VMEM,
        out_shape=jax.ShapeDtypeStruct(total.shape, total.dtype),
        compiler_params=pltpu.CompilerParams(vmem_limit_bytes=2 * MIB),
        name="join",
    )(total, received, after)


def exchange(total, bit):
    devices = lax.axis_size("ctx")
    return lax.ppermute(total, "ctx", [(device, device ^ 2**bit) for device in range(devices)])


def body(queries, key_vectors, value_vectors, token_rows, weight_table):
    table_rows, head_count, level_count = weight_table.shape
    token_count = queries.shape[0]
    width = queries.shape[1] // head_count
    block_count = token_count // BLOCK
    local_bits = token_count.bit_length() - 1
    devices = lax.axis_size("ctx")
    bit_count = devices.bit_length() - 1
    group = head_count // GROUPS
    shape = jax.ShapeDtypeStruct
    whole = shape(queries.shape, queries.dtype)
    params = pltpu.CompilerParams(vmem_limit_bytes=8 * MIB)
    in_hbm = lambda array: pltpu.with_memory_space_constraint(array, pltpu.HBM)
    queries, key_vectors, value_vectors = in_hbm(queries), in_hbm(key_vectors), in_hbm(value_vectors)

    keys, turned, lefts, *totals = pl.pallas_call(
        totals_kernel,
        in_specs=[HBM] * 2,
        out_specs=[VMEM] * (3 + GROUPS),
        out_shape=[
            whole,
            shape((head_count, width, token_count), jnp.bfloat16),
            shape((head_count, block_count, width, width), jnp.bfloat16),
            *[shape((group, width, width), jnp.float32)] * GROUPS,
        ],
        scratch_shapes=[
            pltpu.VMEM(queries.shape, queries.dtype),
            pltpu.SemaphoreType.DMA((PIECES, 2)),
        ],
        compiler_params=params,
        name="totals",
    )(key_vectors, value_vectors)

    weights, query = pl.pallas_call(
        lambda *refs: prepare_kernel(local_bits, *refs),
        in_specs=[ANY] + [HBM] * 3,
        out_specs=[VMEM] * 2,
        out_shape=[shape((head_count * SLOT, token_count), jnp.float32), whole],
        scratch_shapes=[
            pltpu.VMEM((1, token_count), jnp.int32),
            pltpu.VMEM((level_count, head_count, table_rows), jnp.float32),
            pltpu.SemaphoreType.DMA((3,)),
        ],
        compiler_params=params,
        name="prepare",
    )(lefts, queries, in_hbm(token_rows[None, :]), in_hbm(jnp.transpose(weight_table, (2, 1, 0))))

    received = [[exchange(total, 0)] for total in totals]
    parts = []
    after = weights
    for index, total in enumerate(totals):
        for bit in range(1, bit_count):
            total = join(total, received[index][-1], after)
            received[index].append(exchange(total, bit))
        for head in range(index * group, (index + 1) * group):
            parts += pl.pallas_call(
                lambda *refs, head=head: local_kernel(head, head % group, local_bits, *refs),
                in_specs=[VMEM] * (5 + bit_count - 1),
                out_specs=[VMEM],
                out_shape=[shape((width, token_count), jnp.float32)],
                scratch_shapes=[pltpu.VMEM((2 * block_count, TILES, HALF), jnp.float32)],
                compiler_params=params,
                name="local",
            )(query, keys, turned, lefts, weights, *received[index][:-1])
        after = parts[0]

    out = None
    for index, arrived in enumerate(received):
        heads = tuple(range(index * group, (index + 1) * group))
        operands = [weights, query] + [parts[head] for head in heads] + [arrived[-1]]
        out = pl.pallas_call(
            lambda *refs, heads=heads: remote_kernel(heads, local_bits + bit_count, *refs),
            in_specs=[VMEM] * len(operands) + ([] if out is None else [HBM]),
            out_specs=HBM,
            out_shape=whole,
            input_output_aliases={} if out is None else {len(operands): 0},
            scratch_shapes=[
                pltpu.VMEM((token_count, group * width), jnp.bfloat16),
                pltpu.SemaphoreType.DMA((PIECES,)),
            ],
            compiler_params=params,
            name="remote",
        )(*operands, *(() if out is None else (out,)))
    return out


def solution(mesh):
    placed = (
        P(("groups", "ctx"), "head"),
        P(("groups", "ctx"), "head"),
        P(("groups", "ctx"), "head"),
        P(("groups", "ctx")),
        P(None, "head", None),
    )
    return jax.shard_map(
        body, mesh=mesh, in_specs=placed, out_specs=P(("groups", "ctx"), "head"), check_vma=False
    )
```

```python
import jax
import jax.numpy as jnp
from jax import lax
from jax.experimental import pallas as pl
from jax.experimental.pallas import tpu as pltpu
from jax.sharding import PartitionSpec as P

BLOCK = 256
HALF = BLOCK // 2
BLOCK_BITS = BLOCK.bit_length() - 1
ROWS = 8
ROW_BITS = ROWS.bit_length() - 1
TILES = HALF // ROWS
LANES = 128
SLOT = 32
PIECES = 8
GROUPS = 2
DEPTH = 3
MIB = 1 << 20
VMEM = pl.BlockSpec(memory_space=pltpu.VMEM)
HBM = pl.BlockSpec(memory_space=pltpu.HBM)
ANY = pl.BlockSpec(memory_space=pl.ANY)
ROW_BY_ROW = (((1,), (1,)), ((), ()))


def level_weights(rows_ref, table_ref, weight_ref, local_bits):
    levels, heads, table_rows = table_ref.shape
    device = lax.axis_index("ctx")
    level = lax.broadcasted_iota(jnp.int32, (levels, table_rows), 0)
    scale = jnp.ones((levels, table_rows), jnp.float32)
    for level_id in range(2, levels):
        scale = jnp.where(level == level_id, 2.0 ** (-(level_id - 1) / 2), scale)
    for bit in range(lax.axis_size("ctx").bit_length() - 1):
        held = (device >> bit & 1).astype(jnp.float32)
        scale = jnp.where(level == local_bits + 1 + bit, scale * held, scale)
    slots = []
    for head in range(heads):
        slots.append(table_ref[:, head, :] * scale)
        slots.append(jnp.zeros((SLOT - levels, table_rows), jnp.float32))
    table = jnp.concatenate(slots, axis=0)
    high = table.astype(jnp.bfloat16)
    low = (table - high.astype(jnp.float32)).astype(jnp.bfloat16)
    ids = lax.broadcasted_iota(jnp.int32, (table_rows, BLOCK), 0)
    for start in range(0, weight_ref.shape[1], BLOCK):
        pick = (ids == rows_ref[:, start : start + BLOCK]).astype(jnp.float32).astype(jnp.bfloat16)
        weight_ref[:, start : start + BLOCK] = jnp.dot(
            high, pick, preferred_element_type=jnp.float32
        ) + jnp.dot(low, pick, preferred_element_type=jnp.float32)


def pipelined(units, begin, finish, depth=1):
    begun = [begin(unit) for unit in units[:depth]]
    for index, unit in enumerate(units):
        if index + depth < len(units):
            begun.append(begin(units[index + depth]))
        finish(unit, begun[index])


def totals_kernel(key_hbm, value_hbm, key_ref, turned_ref, left_ref, *refs):
    total_refs = refs[:GROUPS]
    value_ref, sems = refs[GROUPS:]
    token_count = key_ref.shape[0]
    head_count = turned_ref.shape[0]
    group = head_count // GROUPS
    block_count = token_count // BLOCK
    size = token_count // PIECES
    blocks = block_count // PIECES
    copies = []
    for piece in range(PIECES):
        rows = pl.ds(piece * size, size)
        copies.append([
            pltpu.make_async_copy(source.at[rows, :], target.at[rows, :], sems.at[piece, which])
            for which, (source, target) in enumerate(((key_hbm, key_ref), (value_hbm, value_ref)))
        ])
    for pair in copies:
        for copy in pair:
            copy.start()

    held = [{} for _ in range(head_count)]

    def begin(unit):
        block, head = unit
        rows = slice(block * BLOCK, (block + 1) * BLOCK)
        turned = jnp.transpose(value_ref[rows, head * LANES : (head + 1) * LANES])
        turned_ref[head, :, rows] = turned
        return turned

    def finish(unit, turned):
        block, head = unit
        rows = slice(block * BLOCK, (block + 1) * BLOCK)
        carry = jnp.dot(
            turned, key_ref[rows, head * LANES : (head + 1) * LANES], preferred_element_type=jnp.float32
        )
        bit = 0
        while block >> bit & 1:
            carry = carry + held[head].pop(bit)
            bit += 1
        held[head][bit] = carry
        if block + 1 < block_count:
            left_ref[head, block] = carry.astype(jnp.bfloat16)
        else:
            total_refs[head // group][head % group] = carry

    for piece, pair in enumerate(copies):
        for copy in pair:
            copy.wait()
        span = range(piece * blocks, (piece + 1) * blocks)
        pipelined([(block, head) for block in span for head in range(head_count)], begin, finish)


def prepare_kernel(local_bits, after_ref, query_hbm, rows_hbm, table_hbm, weight_ref, query_ref, *refs):
    rows_ref, table_ref, sems = refs
    small = [
        pltpu.make_async_copy(rows_hbm, rows_ref, sems.at[0]),
        pltpu.make_async_copy(table_hbm, table_ref, sems.at[1]),
    ]
    large = pltpu.make_async_copy(query_hbm, query_ref, sems.at[2])
    for copy in small + [large]:
        copy.start()
    for copy in small:
        copy.wait()
    level_weights(rows_ref, table_ref, weight_ref, local_bits)
    large.wait()


def local_kernel(head, place, local_bits, last_level, *refs):
    query_ref, key_ref, turned_ref, left_ref, weight_ref = refs[:5]
    state_refs = refs[5:-3]
    part_ref, ahead_ref, tile_ref = refs[-3:]
    token_count = query_ref.shape[0]
    block_count = token_count // BLOCK
    columns = slice(head * LANES, (head + 1) * LANES)
    base = head * SLOT
    states = [(local_bits + 1 + bit, ref[place].astype(jnp.bfloat16)) for bit, ref in enumerate(state_refs)]

    lane = lax.broadcasted_iota(jnp.int32, (ROWS, HALF), 1)
    source = lax.broadcasted_iota(jnp.int32, (ROWS, HALF), 0)
    lane_tile = lane >> ROW_BITS
    near = (lane & ROWS - 1) ^ source
    behind = source > (lane & ROWS - 1)
    far_tile = lax.broadcasted_iota(jnp.int32, (TILES, HALF), 1) >> ROW_BITS
    far_source = lax.broadcasted_iota(jnp.int32, (TILES, HALF), 0)
    far = far_tile ^ far_source
    far_behind = far_source > far_tile

    def level_row(level, first, count):
        return weight_ref[base + level : base + level + 1, first : first + count]

    def own_half(scores, first, slot):
        chosen = jnp.broadcast_to(level_row(0, first, HALF), (ROWS, HALF))
        for bit in range(ROW_BITS):
            chosen = jnp.where(near >= 2**bit, level_row(1 + bit, first, HALF), chosen)
        chosen = jnp.where(behind, 0.0, chosen)
        spread = jnp.zeros((TILES, HALF), jnp.float32)
        for bit in range(BLOCK_BITS - 1 - ROW_BITS):
            spread = jnp.where(far >= 2**bit, level_row(1 + ROW_BITS + bit, first, HALF), spread)
        tile_ref[slot] = jnp.where(far_behind, 0.0, spread)
        rows = []
        for tile in range(TILES):
            weights = jnp.where(lane_tile == tile, chosen, tile_ref[slot, tile : tile + 1, :])
            rows.append(scores[tile * ROWS : (tile + 1) * ROWS] * weights)
        return jnp.concatenate(rows, axis=0).astype(jnp.bfloat16)

    def scaled(query, level, start):
        return (query.astype(jnp.float32) * level_row(level, start, BLOCK)).astype(jnp.bfloat16)

    def begin(block):
        rows = slice(block * BLOCK, (block + 1) * BLOCK)
        query = jnp.transpose(query_ref[rows, columns])
        return query, jnp.dot(key_ref[rows, columns], query, preferred_element_type=jnp.float32)

    def finish(block, begun):
        query, scores = begun
        start = block * BLOCK
        rows = slice(start, start + BLOCK)
        low = own_half(scores[:HALF, :HALF], start, 2 * block)
        high = own_half(scores[HALF:, HALF:], start + HALF, 2 * block + 1)
        across = (scores[:HALF, HALF:] * level_row(BLOCK_BITS, start + HALF, HALF)).astype(jnp.bfloat16)
        right = [
            jnp.concatenate([low, across], axis=1),
            jnp.concatenate([jnp.zeros_like(low), high], axis=1),
        ]
        left = [turned_ref[head, :, rows]]
        terms = [
            (BLOCK_BITS + 1 + bit, left_ref[head, (block >> bit << bit) - 1])
            for bit in range(block_count.bit_length() - 1)
            if block >> bit & 1
        ]
        for level, sibling in terms + states:
            right.append(scaled(query, level, start))
            left.append(sibling)
        ahead_ref[:, rows] = scaled(query, last_level, start)
        part_ref[:, rows] = jnp.dot(
            jnp.concatenate(left, axis=1), jnp.concatenate(right, axis=0),
            preferred_element_type=jnp.float32,
        )

    pipelined(list(range(block_count)), begin, finish, DEPTH)


def remote_kernel(heads, *refs):
    count = len(heads)
    part_refs = refs[:count]
    ahead_refs = refs[count : 2 * count]
    state_ref = refs[2 * count]
    out_hbm, buffer, sems = refs[-3:]
    token_count = buffer.shape[0]
    size = token_count // PIECES
    states = [state_ref[place].astype(jnp.bfloat16) for place in range(count)]
    copies = []

    def begin(unit):
        start, place = unit
        return jnp.dot(
            states[place], ahead_refs[place][:, start : start + BLOCK], preferred_element_type=jnp.float32
        )

    def finish(unit, product):
        start, place = unit
        rows = slice(start, start + BLOCK)
        result = part_refs[place][:, rows] + product
        buffer[rows, place * LANES : (place + 1) * LANES] = jnp.transpose(result.astype(buffer.dtype))
        if place + 1 == count and (start + BLOCK) % size == 0:
            piece = pl.ds(start + BLOCK - size, size)
            target = out_hbm.at[piece, pl.ds(heads[0] * LANES, count * LANES)]
            copies.append(pltpu.make_async_copy(buffer.at[piece, :], target, sems.at[len(copies)]))
            copies[-1].start()

    units = [(start, place) for start in range(0, token_count, BLOCK) for place in range(count)]
    pipelined(units, begin, finish)
    for copy in copies:
        copy.wait()


def join_kernel(left_ref, right_ref, after_ref, out_ref):
    out_ref[...] = left_ref[...] + right_ref[...]


def join(total, received, after):
    return pl.pallas_call(
        join_kernel,
        in_specs=[VMEM, VMEM, ANY],
        out_specs=VMEM,
        out_shape=jax.ShapeDtypeStruct(total.shape, total.dtype),
        compiler_params=pltpu.CompilerParams(vmem_limit_bytes=2 * MIB),
        name="join",
    )(total, received, after)


def exchange(total, bit):
    devices = lax.axis_size("ctx")
    return lax.ppermute(total, "ctx", [(device, device ^ 2**bit) for device in range(devices)])


def body(queries, key_vectors, value_vectors, token_rows, weight_table):
    table_rows, head_count, level_count = weight_table.shape
    token_count = queries.shape[0]
    width = queries.shape[1] // head_count
    block_count = token_count // BLOCK
    local_bits = token_count.bit_length() - 1
    devices = lax.axis_size("ctx")
    bit_count = devices.bit_length() - 1
    group = head_count // GROUPS
    shape = jax.ShapeDtypeStruct
    whole = shape(queries.shape, queries.dtype)
    params = pltpu.CompilerParams(vmem_limit_bytes=8 * MIB)
    in_hbm = lambda array: pltpu.with_memory_space_constraint(array, pltpu.HBM)
    queries, key_vectors, value_vectors = in_hbm(queries), in_hbm(key_vectors), in_hbm(value_vectors)

    keys, turned, lefts, *totals = pl.pallas_call(
        totals_kernel,
        in_specs=[HBM] * 2,
        out_specs=[VMEM] * (3 + GROUPS),
        out_shape=[
            whole,
            shape((head_count, width, token_count), jnp.bfloat16),
            shape((head_count, block_count, width, width), jnp.bfloat16),
            *[shape((group, width, width), jnp.float32)] * GROUPS,
        ],
        scratch_shapes=[
            pltpu.VMEM(queries.shape, queries.dtype),
            pltpu.SemaphoreType.DMA((PIECES, 2)),
        ],
        compiler_params=params,
        name="totals",
    )(key_vectors, value_vectors)

    weights, query = pl.pallas_call(
        lambda *refs: prepare_kernel(local_bits, *refs),
        in_specs=[ANY] + [HBM] * 3,
        out_specs=[VMEM] * 2,
        out_shape=[shape((head_count * SLOT, token_count), jnp.float32), whole],
        scratch_shapes=[
            pltpu.VMEM((1, token_count), jnp.int32),
            pltpu.VMEM((level_count, head_count, table_rows), jnp.float32),
            pltpu.SemaphoreType.DMA((3,)),
        ],
        compiler_params=params,
        name="prepare",
    )(lefts, queries, in_hbm(token_rows[None, :]), in_hbm(jnp.transpose(weight_table, (2, 1, 0))))

    received = [[exchange(total, 0)] for total in totals]
    parts, aheads = [], []
    for index, total in enumerate(totals):
        for bit in range(1, bit_count):
            total = join(total, received[index][-1], weights)
            received[index].append(exchange(total, bit))
        for head in range(index * group, (index + 1) * group):
            results = pl.pallas_call(
                lambda *refs, head=head: local_kernel(head, head % group, local_bits, local_bits + bit_count, *refs),
                in_specs=[VMEM] * (5 + bit_count - 1),
                out_specs=[VMEM] * 2,
                out_shape=[
                    shape((width, token_count), jnp.float32),
                    shape((width, token_count), jnp.bfloat16),
                ],
                scratch_shapes=[pltpu.VMEM((2 * block_count, TILES, HALF), jnp.float32)],
                compiler_params=params,
                name="local",
            )(query, keys, turned, lefts, weights, *received[index][:-1])
            parts.append(results[0])
            aheads.append(results[1])

    out = None
    for index, arrived in enumerate(received):
        heads = tuple(range(index * group, (index + 1) * group))
        operands = [parts[head] for head in heads] + [aheads[head] for head in heads] + [arrived[-1]]
        out = pl.pallas_call(
            lambda *refs, heads=heads: remote_kernel(heads, *refs),
            in_specs=[VMEM] * len(operands) + ([] if out is None else [HBM]),
            out_specs=HBM,
            out_shape=whole,
            input_output_aliases={} if out is None else {len(operands): 0},
            scratch_shapes=[
                pltpu.VMEM((token_count, group * width), jnp.bfloat16),
                pltpu.SemaphoreType.DMA((PIECES,)),
            ],
            compiler_params=params,
            name="remote",
        )(*operands, *(() if out is None else (out,)))
    return out


def solution(mesh):
    placed = (
        P(("groups", "ctx"), "head"),
        P(("groups", "ctx"), "head"),
        P(("groups", "ctx"), "head"),
        P(("groups", "ctx")),
        P(None, "head", None),
    )
    return jax.shard_map(
        body, mesh=mesh, in_specs=placed, out_specs=P(("groups", "ctx"), "head"), check_vma=False
    )
```

```python
import jax
import jax.numpy as jnp
from jax import lax
from jax.experimental import pallas as pl
from jax.experimental.pallas import tpu as pltpu
from jax.sharding import PartitionSpec as P

BLOCK = 256
HALF = BLOCK // 2
BLOCK_BITS = BLOCK.bit_length() - 1
ROWS = 8
ROW_BITS = ROWS.bit_length() - 1
TILES = HALF // ROWS
LANES = 128
SLOT = 32
PIECES = 8
GROUPS = 2
DEPTH = 3
MIB = 1 << 20
VMEM = pl.BlockSpec(memory_space=pltpu.VMEM)
HBM = pl.BlockSpec(memory_space=pltpu.HBM)
ANY = pl.BlockSpec(memory_space=pl.ANY)
ROW_BY_ROW = (((1,), (1,)), ((), ()))


def level_weights(rows_ref, table_ref, weight_ref, local_bits):
    levels, heads, table_rows = table_ref.shape
    device = lax.axis_index("ctx")
    level = lax.broadcasted_iota(jnp.int32, (levels, table_rows), 0)
    scale = jnp.ones((levels, table_rows), jnp.float32)
    for level_id in range(2, levels):
        scale = jnp.where(level == level_id, 2.0 ** (-(level_id - 1) / 2), scale)
    for bit in range(lax.axis_size("ctx").bit_length() - 1):
        held = (device >> bit & 1).astype(jnp.float32)
        scale = jnp.where(level == local_bits + 1 + bit, scale * held, scale)
    slots = []
    for head in range(heads):
        slots.append(table_ref[:, head, :] * scale)
        slots.append(jnp.zeros((SLOT - levels, table_rows), jnp.float32))
    table = jnp.concatenate(slots, axis=0)
    high = table.astype(jnp.bfloat16)
    low = (table - high.astype(jnp.float32)).astype(jnp.bfloat16)
    ids = lax.broadcasted_iota(jnp.int32, (table_rows, BLOCK), 0)
    for start in range(0, weight_ref.shape[1], BLOCK):
        pick = (ids == rows_ref[:, start : start + BLOCK]).astype(jnp.float32).astype(jnp.bfloat16)
        weight_ref[:, start : start + BLOCK] = jnp.dot(
            high, pick, preferred_element_type=jnp.float32
        ) + jnp.dot(low, pick, preferred_element_type=jnp.float32)


def pipelined(units, begin, finish, depth=1):
    begun = [begin(unit) for unit in units[:depth]]
    for index, unit in enumerate(units):
        if index + depth < len(units):
            begun.append(begin(units[index + depth]))
        finish(unit, begun[index])


def totals_kernel(key_hbm, value_hbm, key_ref, turned_ref, left_ref, *refs):
    total_refs = refs[:GROUPS]
    value_ref, sems = refs[GROUPS:]
    token_count = key_ref.shape[0]
    head_count = turned_ref.shape[0]
    group = head_count // GROUPS
    block_count = token_count // BLOCK
    size = token_count // PIECES
    blocks = block_count // PIECES
    copies = []
    for piece in range(PIECES):
        rows = pl.ds(piece * size, size)
        copies.append([
            pltpu.make_async_copy(source.at[rows, :], target.at[rows, :], sems.at[piece, which])
            for which, (source, target) in enumerate(((key_hbm, key_ref), (value_hbm, value_ref)))
        ])
    for pair in copies:
        for copy in pair:
            copy.start()

    held = [{} for _ in range(head_count)]

    def begin(unit):
        block, head = unit
        rows = slice(block * BLOCK, (block + 1) * BLOCK)
        turned = jnp.transpose(value_ref[rows, head * LANES : (head + 1) * LANES])
        turned_ref[head, block] = turned
        return turned

    def finish(unit, turned):
        block, head = unit
        rows = slice(block * BLOCK, (block + 1) * BLOCK)
        carry = jnp.dot(
            turned, key_ref[rows, head * LANES : (head + 1) * LANES], preferred_element_type=jnp.float32
        )
        bit = 0
        while block >> bit & 1:
            carry = carry + held[head].pop(bit)
            bit += 1
        held[head][bit] = carry
        if block + 1 < block_count:
            left_ref[head, block] = carry.astype(jnp.bfloat16)
        else:
            total_refs[head // group][head % group] = carry

    for piece, pair in enumerate(copies):
        for copy in pair:
            copy.wait()
        span = range(piece * blocks, (piece + 1) * blocks)
        pipelined([(block, head) for block in span for head in range(head_count)], begin, finish)


def prepare_kernel(local_bits, after_ref, query_hbm, rows_hbm, table_hbm, weight_ref, query_ref, *refs):
    rows_ref, table_ref, sems = refs
    small = [
        pltpu.make_async_copy(rows_hbm, rows_ref, sems.at[0]),
        pltpu.make_async_copy(table_hbm, table_ref, sems.at[1]),
    ]
    large = pltpu.make_async_copy(query_hbm, query_ref, sems.at[2])
    for copy in small + [large]:
        copy.start()
    for copy in small:
        copy.wait()
    level_weights(rows_ref, table_ref, weight_ref, local_bits)
    large.wait()


def local_kernel(head, place, local_bits, *refs):
    query_ref, key_ref, turned_ref, left_ref, weight_ref = refs[:5]
    state_refs = refs[5:-2]
    part_ref, tile_ref = refs[-2:]
    token_count = query_ref.shape[0]
    block_count = token_count // BLOCK
    columns = slice(head * LANES, (head + 1) * LANES)
    base = head * SLOT
    states = [(local_bits + 1 + bit, ref[place].astype(jnp.bfloat16)) for bit, ref in enumerate(state_refs)]

    lane = lax.broadcasted_iota(jnp.int32, (ROWS, HALF), 1)
    source = lax.broadcasted_iota(jnp.int32, (ROWS, HALF), 0)
    lane_tile = lane >> ROW_BITS
    near = (lane & ROWS - 1) ^ source
    behind = source > (lane & ROWS - 1)
    far_tile = lax.broadcasted_iota(jnp.int32, (TILES, HALF), 1) >> ROW_BITS
    far_source = lax.broadcasted_iota(jnp.int32, (TILES, HALF), 0)
    far = far_tile ^ far_source
    far_behind = far_source > far_tile

    def level_row(level, first, count):
        return weight_ref[base + level : base + level + 1, first : first + count]

    def own_half(scores, first, slot):
        chosen = jnp.broadcast_to(level_row(0, first, HALF), (ROWS, HALF))
        for bit in range(ROW_BITS):
            chosen = jnp.where(near >= 2**bit, level_row(1 + bit, first, HALF), chosen)
        chosen = jnp.where(behind, 0.0, chosen)
        spread = jnp.zeros((TILES, HALF), jnp.float32)
        for bit in range(BLOCK_BITS - 1 - ROW_BITS):
            spread = jnp.where(far >= 2**bit, level_row(1 + ROW_BITS + bit, first, HALF), spread)
        tile_ref[slot] = jnp.where(far_behind, 0.0, spread)
        rows = []
        for tile in range(TILES):
            weights = jnp.where(lane_tile == tile, chosen, tile_ref[slot, tile : tile + 1, :])
            rows.append(scores[tile * ROWS : (tile + 1) * ROWS] * weights)
        return jnp.concatenate(rows, axis=0).astype(jnp.bfloat16)

    def begin(block):
        rows = slice(block * BLOCK, (block + 1) * BLOCK)
        query = jnp.transpose(query_ref[rows, columns])
        return query, jnp.dot(key_ref[rows, columns], query, preferred_element_type=jnp.float32)

    def finish(block, begun):
        query, scores = begun
        start = block * BLOCK
        rows = slice(start, start + BLOCK)
        low = own_half(scores[:HALF, :HALF], start, 2 * block)
        high = own_half(scores[HALF:, HALF:], start + HALF, 2 * block + 1)
        across = (scores[:HALF, HALF:] * level_row(BLOCK_BITS, start + HALF, HALF)).astype(jnp.bfloat16)
        right = [
            jnp.concatenate([low, across], axis=1),
            jnp.concatenate([jnp.zeros_like(low), high], axis=1),
        ]
        left = [turned_ref[head, block]]
        terms = [
            (BLOCK_BITS + 1 + bit, left_ref[head, (block >> bit << bit) - 1])
            for bit in range(block_count.bit_length() - 1)
            if block >> bit & 1
        ]
        for level, sibling in terms + states:
            scaled = query.astype(jnp.float32) * level_row(level, start, BLOCK)
            right.append(scaled.astype(jnp.bfloat16))
            left.append(sibling)
        part_ref[block] = jnp.dot(
            jnp.concatenate(left, axis=1), jnp.concatenate(right, axis=0),
            preferred_element_type=jnp.float32,
        )

    pipelined(list(range(block_count)), begin, finish, DEPTH)


def remote_kernel(heads, level, *refs):
    count = len(heads)
    weight_ref, query_ref = refs[:2]
    part_refs = refs[2 : 2 + count]
    state_ref = refs[2 + count]
    out_hbm, buffer, sems = refs[-3:]
    token_count = weight_ref.shape[1]
    size = token_count // PIECES
    states = [state_ref[place].astype(jnp.bfloat16) for place in range(count)]
    copies = []

    def begin(unit):
        start, place = unit
        columns = slice(heads[place] * LANES, (heads[place] + 1) * LANES)
        return lax.dot_general(
            states[place], query_ref[start : start + BLOCK, columns], ROW_BY_ROW,
            preferred_element_type=jnp.float32,
        )

    def finish(unit, product):
        start, place = unit
        rows = slice(start, start + BLOCK)
        row = heads[place] * SLOT + level
        result = part_refs[place][start // BLOCK] + product * weight_ref[row : row + 1, rows]
        buffer[rows, place * LANES : (place + 1) * LANES] = jnp.transpose(result.astype(buffer.dtype))
        if place + 1 == count and (start + BLOCK) % size == 0:
            piece = pl.ds(start + BLOCK - size, size)
            target = out_hbm.at[piece, pl.ds(heads[0] * LANES, count * LANES)]
            copies.append(pltpu.make_async_copy(buffer.at[piece, :], target, sems.at[len(copies)]))
            copies[-1].start()

    units = [(start, place) for start in range(0, token_count, BLOCK) for place in range(count)]
    pipelined(units, begin, finish)
    for copy in copies:
        copy.wait()


def join_kernel(left_ref, right_ref, after_ref, out_ref):
    out_ref[...] = left_ref[...] + right_ref[...]


def join(total, received, after):
    return pl.pallas_call(
        join_kernel,
        in_specs=[VMEM, VMEM, ANY],
        out_specs=VMEM,
        out_shape=jax.ShapeDtypeStruct(total.shape, total.dtype),
        compiler_params=pltpu.CompilerParams(vmem_limit_bytes=2 * MIB),
        name="join",
    )(total, received, after)


def exchange(total, bit):
    devices = lax.axis_size("ctx")
    return lax.ppermute(total, "ctx", [(device, device ^ 2**bit) for device in range(devices)])


def body(queries, key_vectors, value_vectors, token_rows, weight_table):
    table_rows, head_count, level_count = weight_table.shape
    token_count = queries.shape[0]
    width = queries.shape[1] // head_count
    block_count = token_count // BLOCK
    local_bits = token_count.bit_length() - 1
    devices = lax.axis_size("ctx")
    bit_count = devices.bit_length() - 1
    group = head_count // GROUPS
    shape = jax.ShapeDtypeStruct
    whole = shape(queries.shape, queries.dtype)
    params = pltpu.CompilerParams(vmem_limit_bytes=8 * MIB)
    in_hbm = lambda array: pltpu.with_memory_space_constraint(array, pltpu.HBM)
    queries, key_vectors, value_vectors = in_hbm(queries), in_hbm(key_vectors), in_hbm(value_vectors)

    keys, turned, lefts, *totals = pl.pallas_call(
        totals_kernel,
        in_specs=[HBM] * 2,
        out_specs=[VMEM] * (3 + GROUPS),
        out_shape=[
            whole,
            shape((head_count, block_count, width, BLOCK), jnp.bfloat16),
            shape((head_count, block_count, width, width), jnp.bfloat16),
            *[shape((group, width, width), jnp.float32)] * GROUPS,
        ],
        scratch_shapes=[
            pltpu.VMEM(queries.shape, queries.dtype),
            pltpu.SemaphoreType.DMA((PIECES, 2)),
        ],
        compiler_params=params,
        name="totals",
    )(key_vectors, value_vectors)

    weights, query = pl.pallas_call(
        lambda *refs: prepare_kernel(local_bits, *refs),
        in_specs=[ANY] + [HBM] * 3,
        out_specs=[VMEM] * 2,
        out_shape=[shape((head_count * SLOT, token_count), jnp.float32), whole],
        scratch_shapes=[
            pltpu.VMEM((1, token_count), jnp.int32),
            pltpu.VMEM((level_count, head_count, table_rows), jnp.float32),
            pltpu.SemaphoreType.DMA((3,)),
        ],
        compiler_params=params,
        name="prepare",
    )(lefts, queries, in_hbm(token_rows[None, :]), in_hbm(jnp.transpose(weight_table, (2, 1, 0))))

    received = [[exchange(total, 0)] for total in totals]
    parts = []
    after = weights
    for index, total in enumerate(totals):
        for bit in range(1, bit_count):
            total = join(total, received[index][-1], after)
            received[index].append(exchange(total, bit))
        for head in range(index * group, (index + 1) * group):
            parts += pl.pallas_call(
                lambda *refs, head=head: local_kernel(head, head % group, local_bits, *refs),
                in_specs=[VMEM] * (5 + bit_count - 1),
                out_specs=[VMEM],
                out_shape=[shape((block_count, width, BLOCK), jnp.float32)],
                scratch_shapes=[pltpu.VMEM((2 * block_count, TILES, HALF), jnp.float32)],
                compiler_params=params,
                name="local",
            )(query, keys, turned, lefts, weights, *received[index][:-1])
        after = parts[0]

    out = None
    for index, arrived in enumerate(received):
        heads = tuple(range(index * group, (index + 1) * group))
        operands = [weights, query] + [parts[head] for head in heads] + [arrived[-1]]
        out = pl.pallas_call(
            lambda *refs, heads=heads: remote_kernel(heads, local_bits + bit_count, *refs),
            in_specs=[VMEM] * len(operands) + ([] if out is None else [HBM]),
            out_specs=HBM,
            out_shape=whole,
            input_output_aliases={} if out is None else {len(operands): 0},
            scratch_shapes=[
                pltpu.VMEM((token_count, group * width), jnp.bfloat16),
                pltpu.SemaphoreType.DMA((PIECES,)),
            ],
            compiler_params=params,
            name="remote",
        )(*operands, *(() if out is None else (out,)))
    return out


def solution(mesh):
    placed = (
        P(("groups", "ctx"), "head"),
        P(("groups", "ctx"), "head"),
        P(("groups", "ctx"), "head"),
        P(("groups", "ctx")),
        P(None, "head", None),
    )
    return jax.shard_map(
        body, mesh=mesh, in_specs=placed, out_specs=P(("groups", "ctx"), "head"), check_vma=False
    )
```
